256 devices in a mesh: blk: 16 (over y, x_lo, core), grp: 16 (over z, x_hi).
Axes of the slice: x: 4 (x_hi: 2, x_lo: 2; x = x_hi * 2 + x_lo), y: 4, z: 8, core: 2. Of those that a mesh axis runs over, the one named last changes fastest.
Arguments:
- source_rows: float32 [16, 16, 400, 768], P('blk', 'grp'), may hold values from -2.4 to 2.4
- source_state: float32 [16, 16, 768], P('blk', 'grp'), may hold values from 0.05 to 1
- target_rows: float32 [16, 16, 400, 512], P('blk', 'grp'), may hold values from -12.5 to 12.5
- destination_state: float32 [16, 16, 512], P('blk', 'grp'), may hold values from 0.05 to 1
- positives: int32 [4, 16, 16, 768], P(None, 'blk', 'grp'), may hold values from 0 to 511
- relation_ids: int32 [4, 16, 16], P(None, 'blk', 'grp'), may hold values from 0 to 1
- relations: float32 [2, 400, 400], replicated, may hold values from -0.36 to 1.36
Outputs:
- source_out: float32 [16, 16, 400, 768], P('blk', 'grp')
- source_state_out: float32 [16, 16, 768], P('blk', 'grp')
- target_out: float32 [16, 16, 400, 512], P('blk', 'grp')
- target_state_out: float32 [16, 16, 512], P('blk', 'grp')
- relations_out: float32 [2, 400, 400], replicated
- operator_grads: float32 [2, 2, 400, 400], replicated
The draws below stay inside these ranges and needn't reach their ends.
All inputs are finite; a program needn't handle non-finite values.
Results may differ from the reference program's by a relative error of at most 0.0003.
Values sent between devices are 32-bit elements; how exact they have to be, the bound alone decides.
A program may use at most 64 MiB of HBM per device.

```python
import math
import jax
import jax.numpy as jnp
from jax import lax

EMBED_WIDTH = 400
SOURCE_DEV_ROWS = 768
DEST_BLOCK_ROWS = 512
STEPS = 4
NREL = 2
N_BLK = 16
N_GRP = 16


def pair_fields(key):
    base = jax.random.fold_in(key, 11)
    first_key, second_key = jax.random.split(base)
    source_block = jnp.clip(0.4 * jax.random.normal(first_key, (N_BLK, N_GRP, EMBED_WIDTH, SOURCE_DEV_ROWS), jnp.float32), -2.4, 2.4)
    target_block = jnp.clip(0.4 * jax.random.normal(second_key, (N_BLK, N_GRP, EMBED_WIDTH, DEST_BLOCK_ROWS), jnp.float32), -2.4, 2.4)
    return (source_block, target_block)


def draw_source_rows(key, part):
    return pair_fields(key)[0]


def draw_target_rows(key, part):
    return pair_fields(key)[1]


def draw_relations(key, part):
    noise = jnp.clip(jax.random.normal(jax.random.fold_in(key, 23), (NREL, EMBED_WIDTH, EMBED_WIDTH), jnp.float32), -4.0, 4.0)
    return jnp.eye(EMBED_WIDTH, dtype=jnp.float32)[None] + 0.5 / math.sqrt(EMBED_WIDTH) * noise


def place_ends(array, key, smallest, largest):
    index_at = [jax.random.randint(jax.random.fold_in(key, axis), (), 0, length) for axis, length in enumerate(array.shape)]
    main_axis = array.shape.index(max(array.shape))
    next_to = index_at[:main_axis] + [(index_at[main_axis] + 1) % array.shape[main_axis]] + index_at[main_axis + 1:]
    return array.at[tuple(index_at)].set(smallest).at[tuple(next_to)].set(largest)


def level_of(own_key, dims, cuts, least, top_value):
    gain, own = 1.0, jax.random.fold_in(own_key, 6)
    for position, shards_of in cuts:
        steps = jnp.exp(jax.random.uniform(jax.random.fold_in(own, position), (shards_of,), jnp.float32, least / len(cuts), top_value / len(cuts)))
        gain = gain * jnp.repeat(steps, dims[position] // shards_of).reshape([-1 if axis == position else 1 for axis in range(len(dims))])
    return gain


def setup_inputs(seed: int = 0) -> dict:
    seeds = jax.random.split(jax.random.key(seed), 8)
    return {
        "source_rows": draw_source_rows(jax.random.fold_in(seeds[7], 71), 0),
        "source_state": jnp.clip(jnp.exp(math.log(1.0) - 2.9957323 * jax.random.uniform(seeds[1], (N_BLK, N_GRP, SOURCE_DEV_ROWS), jnp.float32) ** level_of(seeds[1], (N_BLK, N_GRP, SOURCE_DEV_ROWS), ((0, 16), (1, 16)), -0.2, 0.2)), 0.05, 1.0),
        "target_rows": draw_target_rows(jax.random.fold_in(seeds[7], 71), 0),
        "destination_state": jnp.clip(jnp.exp(math.log(1.0) - 2.9957323 * jax.random.uniform(seeds[3], (N_BLK, N_GRP, DEST_BLOCK_ROWS), jnp.float32) ** level_of(seeds[3], (N_BLK, N_GRP, DEST_BLOCK_ROWS), ((0, 16), (1, 16)), -0.2, 0.2)), 0.05, 1.0),
        "positives": place_ends(jax.random.randint(seeds[4], (STEPS, N_BLK, N_GRP, SOURCE_DEV_ROWS), 0, DEST_BLOCK_ROWS), jax.random.fold_in(seeds[4], 1), 0, DEST_BLOCK_ROWS - 1).astype(jnp.int32),
        "relation_ids": place_ends(jax.random.randint(seeds[5], (STEPS, N_BLK, N_GRP), 0, NREL), jax.random.fold_in(seeds[5], 1), 0, NREL - 1).astype(jnp.int32),
        "relations": draw_relations(jax.random.fold_in(seeds[7], 71), 0),
    }


entity_rate = 0.1
operator_rate = 0.01
grad_gain = 6.0

def highest_dot(left, right):
    return jnp.dot(left, right, precision=lax.Precision.HIGHEST, preferred_element_type=jnp.float32)

def adagrad_rows(values, state, gradient):
    state_new = state + lax.optimization_barrier(jnp.mean(gradient * gradient, axis=0))
    return (values - entity_rate * gradient / jnp.sqrt(state_new)[None, :], state_new)

def apply_bucket_step(source_block, source_state, target_block, destination_state, partner, relation_matrix):
    queries = highest_dot(relation_matrix.T, source_block)
    scores = highest_dot(queries.T, target_block)
    highest = lax.optimization_barrier(jnp.max(scores, axis=1, keepdims=True))
    expo = jnp.exp(scores - highest)
    chance = expo / lax.optimization_barrier(jnp.sum(expo, axis=1, keepdims=True))
    columns = jnp.arange(target_block.shape[1], dtype=jnp.int32)
    onehot = (columns[None, :] == partner[:, None]).astype(jnp.float32)
    score_grad = chance - onehot
    target_grad = highest_dot(queries, score_grad)
    query_grad = highest_dot(target_block, score_grad.T)
    source_grad = highest_dot(relation_matrix, query_grad)
    relation_matrix_gradient = highest_dot(source_block, query_grad.T)
    source_new, source_state_new = adagrad_rows(source_block, source_state, source_grad)
    target_new, target_state_new = adagrad_rows(target_block, destination_state, target_grad)
    return (source_new, source_state_new, target_new, target_state_new, relation_matrix_gradient)

def reference(source_rows, source_state, target_rows, destination_state, positives, relation_ids, relations):
    hit_count = N_BLK * N_GRP
    gradient_scale = grad_gain / jnp.sqrt(jnp.float32(SOURCE_DEV_ROWS * hit_count))
    source_block = source_rows.reshape(hit_count, EMBED_WIDTH, SOURCE_DEV_ROWS)
    source_block_state = source_state.reshape(hit_count, SOURCE_DEV_ROWS)
    target_block = target_rows
    target_block_state = destination_state
    relation_matrices = relations
    running_totals = jnp.zeros((NREL, EMBED_WIDTH, EMBED_WIDTH), jnp.float32)
    bucket_results = []
    kinds = jnp.arange(NREL, dtype=jnp.int32)
    for bucket_cell in range(STEPS):
        flattened_target = target_block.reshape(hit_count, EMBED_WIDTH, DEST_BLOCK_ROWS)
        flattened_target_state = target_block_state.reshape(hit_count, DEST_BLOCK_ROWS)
        partner_rows = positives[bucket_cell].reshape(hit_count, SOURCE_DEV_ROWS)
        picked_indices = relation_ids[bucket_cell].reshape(hit_count)

        def single_pair(carry, item):
            src_cols, src_state, tgt_cols, tgt_state, partner, relation_index = item
            relation_matrix = relation_matrices[relation_index]
            out = apply_bucket_step(src_cols, src_state, tgt_cols, tgt_state, partner, relation_matrix)
            chosen = (kinds == relation_index).astype(jnp.float32)
            return (carry + chosen[:, None, None] * out[4][None], out[:4])
        running_totals, refreshed_block = lax.scan(single_pair, running_totals, (source_block, source_block_state, flattened_target, flattened_target_state, partner_rows, picked_indices))
        source_block, source_block_state = (refreshed_block[0], refreshed_block[1])
        target_block = jnp.roll(refreshed_block[2].reshape(N_BLK, N_GRP, EMBED_WIDTH, DEST_BLOCK_ROWS), 1, axis=0)
        target_block_state = jnp.roll(refreshed_block[3].reshape(N_BLK, N_GRP, DEST_BLOCK_ROWS), 1, axis=0)
        if bucket_cell % 2 == 1:
            scaled = gradient_scale * running_totals
            bucket_results.append(scaled)
            relation_matrices = relation_matrices - operator_rate * scaled
            running_totals = jnp.zeros((NREL, EMBED_WIDTH, EMBED_WIDTH), jnp.float32)
    return (source_block.reshape(N_BLK, N_GRP, EMBED_WIDTH, SOURCE_DEV_ROWS), source_block_state.reshape(N_BLK, N_GRP, SOURCE_DEV_ROWS), target_block, target_block_state, relation_matrices, jnp.stack(bucket_results))
```

```python
import functools
import math

import jax
import jax.numpy as jnp
from jax import lax
from jax.experimental import pallas as pl
from jax.experimental.pallas import tpu as pltpu
from jax.sharding import PartitionSpec as P

entity_rate = 0.1
operator_rate = 0.01
grad_gain = 6.0

f32, bf16 = jnp.float32, jnp.bfloat16
MESH = pl.DeviceIdType.MESH

W = 400
S = 768
D = 512
C = 256
STEPS = 4
NX, NY, NZ = 4, 4, 8
MAIN, TAIL, TILES = 150, 8, 320
HALF, P1, P2, P3 = TILES // 2, TILES // 8, TILES // 32, 2
N_EX, N_1, N_2, N_3, N_4, N_5, N_6, N_7, N_ALL = 0, 1, 4, 7, 14, 21, 24, 27, 31


def dot(a, b, ca, cb):
    return lax.dot_general(a, b, (((ca,), (cb,)), ((), ())), preferred_element_type=f32)


def split(v):
    high = v.astype(bf16)
    return high, (v - high.astype(f32)).astype(bf16)


def dot3(ah, al, bh, bl, ca, cb):
    return dot(ah, bh, ca, cb) + (dot(ah, bl, ca, cb) + dot(al, bh, ca, cb))


def dot3_rows(ah, al, bh, bl):
    left = jnp.concatenate([ah, ah, al], axis=0)
    right = jnp.concatenate([bh, bl, bh], axis=0)
    return dot(left, right, 0, 0)


def adagrad(values, state, gradient):
    state_new = state + jnp.sum(gradient * gradient, axis=0, keepdims=True) * (1.0 / W)
    return values - gradient * (entity_rate / jnp.sqrt(state_new)), state_new


def kernel(
    gradient_scale,
    x_in,
    xst_in,
    y_in,
    yst_in,
    pos,
    rid,
    rel_in,
    x,
    xst,
    y_out,
    yst_out,
    rel,
    og_out,
    yin,
    ysend,
    xh,
    xl,
    yh,
    yl,
    qh,
    ql,
    sc,
    sh,
    sl,
    gh,
    gl,
    rh,
    rl,
    acc,
    rx,
    r1,
    b1,
    r2,
    b2,
    r3,
    g3,
    g2,
    gall,
    y_ssem,
    y_rsem,
    ssem,
    rsem,
):
    blk, grp = lax.axis_index("blk"), lax.axis_index("grp")
    core = blk % 2
    my_y = blk // 4
    my_x = (grp % 2) * 2 + (blk // 2) % 2
    my_z = grp // 2
    first = my_x * (1 - core) + my_y * core
    second = my_y * (1 - core) + my_x * core

    def at(px, py, pz, pc):
        return ((py * 2 + px % 2) * 2 + pc, pz * 2 + px // 2)

    def first_peer(p):
        return at(p * (1 - core) + my_x * core, p * core + my_y * (1 - core), my_z, core)

    def second_peer(p):
        return at(p * core + my_x * (1 - core), p * (1 - core) + my_y * core, my_z, core)

    def z_peer(p):
        return at(my_x, my_y, p, core)

    other = at(my_x, my_y, my_z, 1 - core)
    behind = ((blk + 1) % 16, grp)
    far = ((blk + 15 + 2 * core) % 16, grp)

    barrier = pltpu.get_barrier_semaphore()
    peers = [other, far]
    peers += [first_peer((first + j) % 4) for j in range(1, 4)]
    peers += [second_peer((second + j) % 4) for j in range(1, 4)]
    peers += [z_peer((my_z + j) % NZ) for j in range(1, NZ)]
    for peer in peers:
        pl.semaphore_signal(barrier, inc=1, device_id=peer, device_id_type=MESH)

    x[...] = x_in[...]
    xst[...] = xst_in[...]
    rel[...] = rel_in[...]
    xh[...], xl[...] = split(x_in[...])
    rh[...], rl[...] = split(rel_in[...])
    for c in range(2):
        yin[0, c, :W] = y_in[:, c * C : (c + 1) * C]
        yin[0, c, W:] = jnp.broadcast_to(yst_in[:, c * C : (c + 1) * C], (8, C))
    gh[W:] = jnp.zeros((D - W, S), bf16)
    gl[W:] = jnp.zeros((D - W, S), bf16)
    acc[2 * MAIN :] = jnp.zeros((TILES - 2 * MAIN, 8, 128), f32)
    b2[P2:] = jnp.zeros((P3 * NZ - P2, 8, 128), f32)

    pl.semaphore_wait(barrier, len(peers))

    def queries(k):
        r = rid[k]
        qh[...], ql[...] = split(dot3_rows(rh[r], rl[r], xh[...], xl[...]))

    def scores(k, arrived):
        for c in range(2):
            if arrived is not None:
                arrived[c].wait_recv()
            high, low = split(yin[k, c, :W])
            yh[:, c * C : (c + 1) * C] = high
            yl[:, c * C : (c + 1) * C] = low
            sc[c * C : (c + 1) * C] = dot3_rows(high, low, qh[...], ql[...])
        for n in range(3):
            part = slice(n * 256, (n + 1) * 256)
            s = sc[:, part]
            e = jnp.exp(s - jnp.max(s, axis=0, keepdims=True))
            chance = e * (1.0 / jnp.sum(e, axis=0, keepdims=True))
            rows = lax.broadcasted_iota(jnp.int32, (D, 256), 0)
            onehot = (rows == pos[k, :, part]).astype(f32)
            sh[:, part], sl[:, part] = split(chance - onehot)

    def new_targets(k, c):
        part = slice(c * C, (c + 1) * C)
        grad = dot3(qh[...], ql[...], sh[part], sl[part], 1, 1)
        rows, state = adagrad(yin[k, c, :W], yin[k, c, W : W + 1], grad)
        ysend[k, c, :W] = rows
        ysend[k, c, W:] = jnp.broadcast_to(state, (8, C))

    def send_targets(k, c):
        copy = pltpu.make_async_remote_copy(
            src_ref=ysend.at[k, c],
            dst_ref=yin.at[k + 1, c],
            send_sem=y_ssem.at[k, c],
            recv_sem=y_rsem.at[k, c],
            device_id=behind,
            device_id_type=MESH,
        )
        copy.start()
        return copy

    def query_grad():
        gh[:W], gl[:W] = split(dot3(yh[...], yl[...], sh[...], sl[...], 1, 0))

    def operator_grad(k, add):
        og = dot3(xh[...], xl[...], gh[...], gl[...], 1, 1)
        tail = og[:, 384:].T[:16]
        for r in range(2):
            mine = (rid[k] == r).astype(f32)
            for c in range(3):
                at_ = pl.ds(r * MAIN + c * 50, 50)
                part = mine * og[:, c * 128 : (c + 1) * 128].reshape(50, 8, 128)
                acc[at_] = acc[at_] + part if add else part
            for i in range(2):
                for c in range(4):
                    n = 128 if c < 3 else 16
                    t = 2 * MAIN + r * TAIL + i * 4 + c
                    part = mine * tail[i * 8 : (i + 1) * 8, c * 128 : c * 128 + n]
                    acc[t, :, :n] = acc[t, :, :n] + part if add else part

    def new_sources(k):
        r = rid[k]
        grad = dot3(rh[r], rl[r], gh[:W], gl[:W], 1, 0)
        rows, state = adagrad(x[...], xst[...], grad)
        x[...] = rows
        xst[...] = state
        xh[...], xl[...] = split(rows)

    def update(u, _):
        def send(number, src, dst, peer):
            copy = pltpu.make_async_remote_copy(
                src_ref=src,
                dst_ref=dst,
                send_sem=ssem.at[u, number],
                recv_sem=rsem.at[u, number],
                device_id=peer,
                device_id_type=MESH,
            )
            copy.start()
            return copy

        k = 2 * u
        queries(k)
        scores(k, None)
        moved = []
        for c in range(2):
            new_targets(k, c)
            moved.append(send_targets(k, c))
        query_grad()
        operator_grad(k, False)
        new_sources(k)
        queries(k + 1)
        scores(k + 1, moved)
        query_grad()
        operator_grad(k + 1, True)

        sent = [send(N_EX, acc.at[pl.ds((1 - core) * HALF, HALF)], rx.at[u], other)]
        new_sources(k + 1)
        sent[0].wait_recv()
        r1[...] = acc[pl.ds(core * HALF, HALF)] + rx[u]
        got = []
        for j in range(1, 4):
            p = (first + j) % 4
            got.append(send(N_1 + j - 1, r1.at[pl.ds(p * P1, P1)], b1.at[u, j - 1], first_peer(p)))
        sent += got
        for c in range(2):
            new_targets(k + 1, c)
        for copy in got:
            copy.wait_recv()
        moved2 = [send_targets(k + 1, c) for c in range(2)]
        r2[...] = r1[pl.ds(first * P1, P1)] + b1[u, 0] + b1[u, 1] + b1[u, 2]
        got = []
        for j in range(1, 4):
            p = (second + j) % 4
            got.append(send(N_2 + j - 1, r2.at[pl.ds(p * P2, P2)], r3.at[u, j - 1], second_peer(p)))
        sent += got
        for copy in got:
            copy.wait_recv()
        b2[:P2] = r2[pl.ds(second * P2, P2)] + r3[u, 0] + r3[u, 1] + r3[u, 2]
        got = []
        for j in range(1, NZ):
            p = (my_z + j) % NZ
            got.append(send(N_3 + j - 1, b2.at[pl.ds(p * P3, P3)], g3.at[u, j], z_peer(p)))
        sent += got
        for copy in got:
            copy.wait_recv()
        total = b2[pl.ds(my_z * P3, P3)]
        for j in range(1, NZ):
            total = total + g3[u, j]
        g3[u, 0] = gradient_scale * total
        mine = pl.ds(my_z * P3, P3)
        g2[u, mine] = g3[u, 0]
        got = []
        for j in range(1, NZ):
            p = (my_z + j) % NZ
            got.append(send(N_4 + j - 1, g3.at[u, 0], g2.at[u, mine], z_peer(p)))
        sent += got
        for copy in got:
            copy.wait_recv()
        mine = pl.ds((core * 4 + first) * P1 + second * P2, P2)
        gall[u, mine] = g2[u, pl.ds(0, P2)]
        got = []
        for j in range(1, 4):
            p = (second + j) % 4
            got.append(send(N_5 + j - 1, g2.at[u, pl.ds(0, P2)], gall.at[u, mine], second_peer(p)))
        sent += got
        for copy in got:
            copy.wait_recv()
        mine = pl.ds((core * 4 + first) * P1, P1)
        got = []
        for j in range(1, 4):
            p = (first + j) % 4
            got.append(send(N_6 + j - 1, gall.at[u, mine], gall.at[u, mine], first_peer(p)))
        sent += got
        across = [send(N_7, gall.at[u, mine], gall.at[u, mine], other)]
        for j in range(1, 4):
            got[j - 1].wait_recv()
            theirs = pl.ds((core * 4 + (first + 4 - j) % 4) * P1, P1)
            across.append(send(N_7 + j, gall.at[u, theirs], gall.at[u, theirs], other))
        sent += across
        for copy in across:
            copy.wait_recv()

        for r in range(2):
            for c in range(3):
                part = gall[u, pl.ds(r * MAIN + c * 50, 50)].reshape(W, 128)
                og_out[u, r, :, c * 128 : (c + 1) * 128] = part
            rows = []
            for i in range(2):
                t = 2 * MAIN + r * TAIL + i * 4
                rows.append(jnp.concatenate([gall[u, t + c] for c in range(4)], axis=1))
            rows.append(jnp.zeros((112, D), f32))
            tail = jnp.concatenate(rows, axis=0).T
            og_out[u, r, :, 384:] = tail[:W, :16]
            rel_new = rel[r] - operator_rate * og_out[u, r]
            rel[r] = rel_new
            rh[r], rl[r] = split(rel_new)
        for copy in moved + moved2:
            copy.wait_send()
        for copy in sent:
            copy.wait_send()
        for copy in moved2:
            copy.wait_recv()
        return 0

    lax.fori_loop(0, STEPS // 2, update, 0)
    for c in range(2):
        y_out[:, c * C : (c + 1) * C] = yin[STEPS, c, :W]
        yst_out[:, c * C : (c + 1) * C] = yin[STEPS, c, W : W + 1]


def shards(
    source_rows, source_state, target_rows, destination_state, positives, relation_ids, relations
):
    everyone = S * lax.axis_size("blk") * lax.axis_size("grp")
    gradient_scale = grad_gain / math.sqrt(everyone)
    vmem = pl.BlockSpec(memory_space=pltpu.VMEM)
    smem = pl.BlockSpec(memory_space=pltpu.SMEM)
    tiles = (8, 128)
    out = pl.pallas_call(
        functools.partial(kernel, gradient_scale),
        out_shape=(
            jax.ShapeDtypeStruct((W, S), f32),
            jax.ShapeDtypeStruct((1, S), f32),
            jax.ShapeDtypeStruct((W, D), f32),
            jax.ShapeDtypeStruct((1, D), f32),
            jax.ShapeDtypeStruct((2, W, W), f32),
            jax.ShapeDtypeStruct((2, 2, W, W), f32),
        ),
        in_specs=[vmem, vmem, vmem, vmem, vmem, smem, vmem],
        out_specs=(vmem,) * 6,
        scratch_shapes=[
            pltpu.VMEM((STEPS + 1, 2, W + 8, C), f32),
            pltpu.VMEM((STEPS, 2, W + 8, C), f32),
            pltpu.VMEM((W, S), bf16),
            pltpu.VMEM((W, S), bf16),
            pltpu.VMEM((W, D), bf16),
            pltpu.VMEM((W, D), bf16),
            pltpu.VMEM((W, S), bf16),
            pltpu.VMEM((W, S), bf16),
            pltpu.VMEM((D, S), f32),
            pltpu.VMEM((D, S), bf16),
            pltpu.VMEM((D, S), bf16),
            pltpu.VMEM((D, S), bf16),
            pltpu.VMEM((D, S), bf16),
            pltpu.VMEM((2, W, W), bf16),
            pltpu.VMEM((2, W, W), bf16),
            pltpu.VMEM((TILES, *tiles), f32),
            pltpu.VMEM((2, HALF, *tiles), f32),
            pltpu.VMEM((HALF, *tiles), f32),
            pltpu.VMEM((2, 3, P1, *tiles), f32),
            pltpu.VMEM((P1, *tiles), f32),
            pltpu.VMEM((P3 * NZ, *tiles), f32),
            pltpu.VMEM((2, 3, P2, *tiles), f32),
            pltpu.VMEM((2, NZ, P3, *tiles), f32),
            pltpu.VMEM((2, P3 * NZ, *tiles), f32),
            pltpu.VMEM((2, TILES, *tiles), f32),
            pltpu.SemaphoreType.DMA((STEPS, 2)),
            pltpu.SemaphoreType.DMA((STEPS, 2)),
            pltpu.SemaphoreType.DMA((2, N_ALL)),
            pltpu.SemaphoreType.DMA((2, N_ALL)),
        ],
        compiler_params=pltpu.CompilerParams(
            collective_id=0, has_side_effects=True, vmem_limit_bytes=58 << 20
        ),
        name="train",
    )(
        source_rows[0, 0],
        source_state[0],
        target_rows[0, 0],
        destination_state[0],
        positives[:, 0],
        relation_ids[:, 0, 0],
        relations,
    )
    source, source_state, target, target_state, relations, grads = out
    return (
        source[None, None],
        source_state[None],
        target[None, None],
        target_state[None],
        relations,
        grads,
    )


def solution(mesh):
    in_specs = (
        P("blk", "grp", None, None),
        P("blk", "grp", None),
        P("blk", "grp", None, None),
        P("blk", "grp", None),
        P(None, "blk", "grp", None),
        P(None, "blk", "grp"),
        P(),
    )
    out_specs = (
        P("blk", "grp", None, None),
        P("blk", "grp", None),
        P("blk", "grp", None, None),
        P("blk", "grp", None),
        P(),
        P(),
    )
    return jax.shard_map(shards, mesh=mesh, in_specs=in_specs, out_specs=out_specs, check_vma=False)
```

```python
import functools
import math

import jax
import jax.numpy as jnp
from jax import lax
from jax.experimental import pallas as pl
from jax.experimental.pallas import tpu as pltpu
from jax.sharding import PartitionSpec as P

entity_rate = 0.1
operator_rate = 0.01
grad_gain = 6.0

f32, bf16 = jnp.float32, jnp.bfloat16
MESH = pl.DeviceIdType.MESH

W = 400
S = 768
D = 512
C = 256
STEPS = 4
NX, NY, NZ = 4, 4, 8
MAIN, TAIL, TILES = 150, 8, 320
PART = 100
HALF, P1, P2, P3 = TILES // 2, TILES // 8, TILES // 32, 2
N_EX, N_1, N_2, N_3, N_4, N_5, N_6, N_7, N_ALL = 0, 2, 5, 8, 15, 22, 25, 28, 32
RING_ORDER = (2, 1, 3)
Z_ORDER = (4, 3, 5, 2, 6, 1, 7)


def dot(a, b, ca, cb):
    return lax.dot_general(a, b, (((ca,), (cb,)), ((), ())), preferred_element_type=f32)


def split(v):
    high = v.astype(bf16)
    return high, (v - high.astype(f32)).astype(bf16)


def dot3(ah, al, bh, bl, ca, cb):
    return dot(ah, bh, ca, cb) + (dot(ah, bl, ca, cb) + dot(al, bh, ca, cb))


def dot3_rows(ah, al, bh, bl):
    left = jnp.concatenate([ah, ah, al], axis=0)
    right = jnp.concatenate([bh, bl, bh], axis=0)
    return dot(left, right, 0, 0)


def adagrad(values, state, gradient):
    state_new = state + jnp.sum(gradient * gradient, axis=0, keepdims=True) * (1.0 / W)
    return values - gradient * (entity_rate / jnp.sqrt(state_new)), state_new


def unpack(gall, u, r, store):
    base = r * HALF
    for c in range(3):
        store(c * 128, (c + 1) * 128, gall[u, pl.ds(base + c * 50, 50)].reshape(W, 128))
    rows = []
    for i in range(2):
        t = base + MAIN + i * 4
        rows.append(jnp.concatenate([gall[u, t + c] for c in range(4)], axis=1))
    rows.append(jnp.zeros((112, D), f32))
    store(384, W, jnp.concatenate(rows, axis=0).T[:W, :16])


def kernel(
    gradient_scale,
    x_in,
    xst_in,
    y_in,
    yst_in,
    pos,
    rid,
    rel_in,
    x_out,
    xst,
    y_out,
    gall_out,
    x,
    y,
    rel,
    yin,
    ysend,
    xh,
    xl,
    yh,
    yl,
    qh,
    ql,
    sc,
    sh,
    sl,
    gh,
    gl,
    rh,
    rl,
    acc,
    rx,
    r1,
    b1,
    r2,
    b2,
    r3,
    g3,
    g2,
    gall,
    y_ssem,
    y_rsem,
    ssem,
    rsem,
    lsem,
):
    blk, grp = lax.axis_index("blk"), lax.axis_index("grp")
    core = blk % 2
    my_y = blk // 4
    my_x = (grp % 2) * 2 + (blk // 2) % 2
    my_z = grp // 2
    first = my_x * (1 - core) + my_y * core
    second = my_y * (1 - core) + my_x * core

    def at(px, py, pz, pc):
        return ((py * 2 + px % 2) * 2 + pc, pz * 2 + px // 2)

    def first_peer(p):
        return at(p * (1 - core) + my_x * core, p * core + my_y * (1 - core), my_z, core)

    def second_peer(p):
        return at(p * core + my_x * (1 - core), p * (1 - core) + my_y * core, my_z, core)

    def z_peer(p):
        return at(my_x, my_y, p, core)

    other = at(my_x, my_y, my_z, 1 - core)
    behind = ((blk + 1) % 16, grp)
    far = ((blk + 15 + 2 * core) % 16, grp)

    barrier = pltpu.get_barrier_semaphore()
    peers = [other, far]
    peers += [first_peer((first + j) % 4) for j in range(1, 4)]
    peers += [second_peer((second + j) % 4) for j in range(1, 4)]
    peers += [z_peer((my_z + j) % NZ) for j in range(1, NZ)]
    for peer in peers:
        pl.semaphore_signal(barrier, inc=1, device_id=peer, device_id_type=MESH)

    loads = [
        pltpu.make_async_copy(src, dst, lsem.at[n])
        for n, (src, dst) in enumerate(((rel_in, rel), (x_in, x), (y_in, y)))
    ]
    for copy in loads:
        copy.start()
    xst[...] = xst_in[...]
    gh[W:] = jnp.zeros((D - W, S), bf16)
    gl[W:] = jnp.zeros((D - W, S), bf16)
    for r in range(2):
        pad = r * HALF + MAIN
        acc[pad : pad + 10] = jnp.zeros((10, 8, 128), f32)
    b2[P2:] = jnp.zeros((P3 * NZ - P2, 8, 128), f32)
    loads[0].wait()
    rh[...], rl[...] = split(rel[...])
    loads[1].wait()
    xh[...], xl[...] = split(x[...])
    loads[2].wait()
    for c in range(2):
        yin[0, c, :W] = y[:, c * C : (c + 1) * C]
        yin[0, c, W:] = jnp.broadcast_to(yst_in[:, c * C : (c + 1) * C], (8, C))

    def queries(k):
        r = rid[k]
        qh[...], ql[...] = split(dot3_rows(rh[r], rl[r], xh[...], xl[...]))

    def scores(k, arrived):
        for c in range(2):
            if arrived is not None:
                arrived[c].wait_recv()
            high, low = split(yin[k, c, :W])
            yh[:, c * C : (c + 1) * C] = high
            yl[:, c * C : (c + 1) * C] = low
            sc[c * C : (c + 1) * C] = dot3_rows(high, low, qh[...], ql[...])
        for n in range(3):
            part = slice(n * 256, (n + 1) * 256)
            s = sc[:, part]
            e = jnp.exp(s - jnp.max(s, axis=0, keepdims=True))
            chance = e * (1.0 / jnp.sum(e, axis=0, keepdims=True))
            rows = lax.broadcasted_iota(jnp.int32, (D, 256), 0)
            onehot = (rows == pos[k, :, part]).astype(f32)
            sh[:, part], sl[:, part] = split(chance - onehot)

    def new_targets(k, c):
        part = slice(c * C, (c + 1) * C)
        grad = dot3(qh[...], ql[...], sh[part], sl[part], 1, 1)
        rows, state = adagrad(yin[k, c, :W], yin[k, c, W : W + 1], grad)
        ysend[k, c, :W] = rows
        ysend[k, c, W:] = jnp.broadcast_to(state, (8, C))

    def send_targets(k, c):
        copy = pltpu.make_async_remote_copy(
            src_ref=ysend.at[k, c],
            dst_ref=yin.at[k + 1, c],
            send_sem=y_ssem.at[k, c],
            recv_sem=y_rsem.at[k, c],
            device_id=behind,
            device_id_type=MESH,
        )
        copy.start()
        return copy

    def query_grad():
        gh[:W], gl[:W] = split(dot3(yh[...], yl[...], sh[...], sl[...], 1, 0))

    def operator_grad(k, h, add):
        part = slice(h * 256, (h + 1) * 256)
        og = dot3(xh[...], xl[...], gh[part], gl[part], 1, 1)
        for r in range(2):
            mine = rid[k] == r
            for c in range(2 - h):
                to = pl.ds(r * HALF + (2 * h + c) * 50, 50)
                new = jnp.where(mine, og[:, c * 128 : (c + 1) * 128].reshape(50, 8, 128), 0.0)
                acc[to] = acc[to] + new if add else new
        if h == 0:
            return
        tail = og[:, 128:].T[:16]
        for r in range(2):
            mine = rid[k] == r
            for i in range(2):
                for c in range(4):
                    n = 128 if c < 3 else 16
                    t = r * HALF + MAIN + i * 4 + c
                    new = jnp.where(mine, tail[i * 8 : (i + 1) * 8, c * 128 : c * 128 + n], 0.0)
                    acc[t, :, :n] = acc[t, :, :n] + new if add else new

    def new_sources(k):
        r = rid[k]
        grad = dot3(rh[r], rl[r], gh[:W], gl[:W], 1, 0)
        rows, state = adagrad(x[...], xst[...], grad)
        x[...] = rows
        xst[...] = state
        xh[...], xl[...] = split(rows)

    def update(u, _):
        def send(number, src, dst, peer):
            copy = pltpu.make_async_remote_copy(
                src_ref=src,
                dst_ref=dst,
                send_sem=ssem.at[u, number],
                recv_sem=rsem.at[u, number],
                device_id=peer,
                device_id_type=MESH,
            )
            copy.start()
            return copy

        k = 2 * u
        queries(k)
        scores(k, None)
        new_targets(k, 0)

        @pl.when(u == 0)
        def _():
            pl.semaphore_wait(barrier, len(peers))

        moved = [send_targets(k, 0)]
        new_targets(k, 1)
        moved.append(send_targets(k, 1))
        query_grad()
        for h in range(2):
            operator_grad(k, h, False)
        new_sources(k)
        queries(k + 1)
        scores(k + 1, moved)
        query_grad()

        sent = []
        for h in range(2):
            operator_grad(k + 1, h, True)
            start, size = (0, PART) if h == 0 else (PART, HALF - PART)
            theirs = pl.ds((1 - core) * HALF + start, size)
            sent.append(send(N_EX + h, acc.at[theirs], rx.at[u, pl.ds(start, size)], other))
        new_sources(k + 1)

        @pl.when(u == 1)
        def _():
            pltpu.make_async_copy(x, x_out, lsem.at[3]).start()

        for copy in sent:
            copy.wait_recv()

        def chip_sum(p):
            r1[pl.ds(p * P1, P1)] = acc[pl.ds(core * HALF + p * P1, P1)] + rx[u, pl.ds(p * P1, P1)]

        got = []
        for j in RING_ORDER:
            p = (first + j) % 4
            chip_sum(p)
            got.append(send(N_1 + j - 1, r1.at[pl.ds(p * P1, P1)], b1.at[u, j - 1], first_peer(p)))
        chip_sum(first)
        sent += got
        for c in range(2):
            new_targets(k + 1, c)
        for copy in got:
            copy.wait_recv()
        r2[...] = r1[pl.ds(first * P1, P1)] + b1[u, 0] + b1[u, 1] + b1[u, 2]
        got = []
        for j in RING_ORDER:
            p = (second + j) % 4
            got.append(send(N_2 + j - 1, r2.at[pl.ds(p * P2, P2)], r3.at[u, j - 1], second_peer(p)))
        sent += got
        moved2 = [send_targets(k + 1, c) for c in range(2)]
        for copy in got:
            copy.wait_recv()
        b2[:P2] = r2[pl.ds(second * P2, P2)] + r3[u, 0] + r3[u, 1] + r3[u, 2]
        got = []
        for j in Z_ORDER:
            p = (my_z + j) % NZ
            got.append(send(N_3 + j - 1, b2.at[pl.ds(p * P3, P3)], g3.at[u, j], z_peer(p)))
        sent += got
        for copy in got:
            copy.wait_recv()
        total = b2[pl.ds(my_z * P3, P3)]
        for j in range(1, NZ):
            total = total + g3[u, j]
        g3[u, 0] = gradient_scale * total
        mine = pl.ds(my_z * P3, P3)
        g2[u, mine] = g3[u, 0]
        got = []
        for j in Z_ORDER:
            p = (my_z + j) % NZ
            got.append(send(N_4 + j - 1, g3.at[u, 0], g2.at[u, mine], z_peer(p)))
        sent += got
        for copy in got:
            copy.wait_recv()
        mine = pl.ds((core * 4 + first) * P1 + second * P2, P2)
        gall[u, mine] = g2[u, pl.ds(0, P2)]
        got = []
        for j in RING_ORDER:
            p = (second + j) % 4
            got.append(send(N_5 + j - 1, g2.at[u, pl.ds(0, P2)], gall.at[u, mine], second_peer(p)))
        sent += got
        for copy in got:
            copy.wait_recv()
        mine = pl.ds((core * 4 + first) * P1, P1)
        got = []
        for j in RING_ORDER:
            p = (first + j) % 4
            got.append(send(N_6 + j - 1, gall.at[u, mine], gall.at[u, mine], first_peer(p)))
        sent += got
        across = [send(N_7, gall.at[u, mine], gall.at[u, mine], other)]
        for n, j in ((1, 1), (2, 3), (0, 2)):
            got[n].wait_recv()
            theirs = pl.ds((core * 4 + (first + 4 - j) % 4) * P1, P1)
            across.append(send(N_7 + j, gall.at[u, theirs], gall.at[u, theirs], other))
        sent += across
        for copy in across:
            copy.wait_recv()

        @pl.when(u == 0)
        def _():
            for r in range(2):

                def store(start, end, values):
                    rel[r, :, start:end] = rel[r, :, start:end] - operator_rate * values

                unpack(gall, u, r, store)
                rh[r], rl[r] = split(rel[r])

        for copy in moved + moved2 + sent:
            copy.wait_send()
        for copy in moved2:
            copy.wait_recv()
        return 0

    lax.fori_loop(0, STEPS // 2, update, 0)
    stores = [
        pltpu.make_async_copy(yin.at[STEPS], y_out, lsem.at[4]),
        pltpu.make_async_copy(gall, gall_out, lsem.at[5]),
    ]
    for copy in stores:
        copy.start()
    for copy in stores:
        copy.wait()
    pltpu.make_async_copy(x, x_out, lsem.at[3]).wait()


def finish(x, xst, yin, gall, rel, x_out, xst_out, y_out, yst_out, rel_out, og_out, sem):
    copy = pltpu.make_async_copy(x, x_out, sem)
    copy.start()
    xst_out[...] = xst[...]
    for c in range(2):
        y_out[:, c * C : (c + 1) * C] = yin[c, :W]
        yst_out[:, c * C : (c + 1) * C] = yin[c, W : W + 1]
    for r in range(2):
        for u in range(2):

            def store(start, end, values):
                og_out[u, r, :, start:end] = values
                before = rel[r, :, start:end] if u == 0 else rel_out[r, :, start:end]
                rel_out[r, :, start:end] = before - operator_rate * values

            unpack(gall, u, r, store)
    copy.wait()


def shards(
    source_rows, source_state, target_rows, destination_state, positives, relation_ids, relations
):
    everyone = S * lax.axis_size("blk") * lax.axis_size("grp")
    gradient_scale = grad_gain / math.sqrt(everyone)
    vmem = pl.BlockSpec(memory_space=pltpu.VMEM)
    smem = pl.BlockSpec(memory_space=pltpu.SMEM)
    hbm = pl.BlockSpec(memory_space=pl.ANY)
    tiles = (8, 128)
    source, source_state, target, grads = pl.pallas_call(
        functools.partial(kernel, gradient_scale),
        out_shape=(
            jax.ShapeDtypeStruct((W, S), f32),
            jax.ShapeDtypeStruct((1, S), f32),
            jax.ShapeDtypeStruct((2, W + 8, C), f32),
            jax.ShapeDtypeStruct((2, TILES, *tiles), f32),
        ),
        in_specs=[hbm, vmem, hbm, vmem, vmem, smem, hbm],
        out_specs=(hbm, vmem, hbm, hbm),
        scratch_shapes=[
            pltpu.VMEM((W, S), f32),
            pltpu.VMEM((W, D), f32),
            pltpu.VMEM((2, W, W), f32),
            pltpu.VMEM((STEPS + 1, 2, W + 8, C), f32),
            pltpu.VMEM((STEPS, 2, W + 8, C), f32),
            pltpu.VMEM((W, S), bf16),
            pltpu.VMEM((W, S), bf16),
            pltpu.VMEM((W, D), bf16),
            pltpu.VMEM((W, D), bf16),
            pltpu.VMEM((W, S), bf16),
            pltpu.VMEM((W, S), bf16),
            pltpu.VMEM((D, S), f32),
            pltpu.VMEM((D, S), bf16),
            pltpu.VMEM((D, S), bf16),
            pltpu.VMEM((D, S), bf16),
            pltpu.VMEM((D, S), bf16),
            pltpu.VMEM((2, W, W), bf16),
            pltpu.VMEM((2, W, W), bf16),
            pltpu.VMEM((TILES, *tiles), f32),
            pltpu.VMEM((2, HALF, *tiles), f32),
            pltpu.VMEM((HALF, *tiles), f32),
            pltpu.VMEM((2, 3, P1, *tiles), f32),
            pltpu.VMEM((P1, *tiles), f32),
            pltpu.VMEM((P3 * NZ, *tiles), f32),
            pltpu.VMEM((2, 3, P2, *tiles), f32),
            pltpu.VMEM((2, NZ, P3, *tiles), f32),
            pltpu.VMEM((2, P3 * NZ, *tiles), f32),
            pltpu.VMEM((2, TILES, *tiles), f32),
            pltpu.SemaphoreType.DMA((STEPS, 2)),
            pltpu.SemaphoreType.DMA((STEPS, 2)),
            pltpu.SemaphoreType.DMA((2, N_ALL)),
            pltpu.SemaphoreType.DMA((2, N_ALL)),
            pltpu.SemaphoreType.DMA((6,)),
        ],
        compiler_params=pltpu.CompilerParams(
            collective_id=0, has_side_effects=True, vmem_limit_bytes=36 << 20
        ),
        name="train",
    )(
        source_rows[0, 0],
        source_state[0],
        target_rows[0, 0],
        destination_state[0],
        positives[:, 0],
        relation_ids[:, 0, 0],
        relations,
    )
    out = pl.pallas_call(
        finish,
        out_shape=(
            jax.ShapeDtypeStruct((W, S), f32),
            jax.ShapeDtypeStruct((1, S), f32),
            jax.ShapeDtypeStruct((W, D), f32),
            jax.ShapeDtypeStruct((1, D), f32),
            jax.ShapeDtypeStruct((2, W, W), f32),
            jax.ShapeDtypeStruct((2, 2, W, W), f32),
        ),
        in_specs=[hbm, vmem, vmem, vmem, vmem],
        out_specs=(hbm, vmem, vmem, vmem, vmem, vmem),
        scratch_shapes=[pltpu.SemaphoreType.DMA],
        compiler_params=pltpu.CompilerParams(vmem_limit_bytes=24 << 20),
        name="finish",
    )(source, source_state, target, grads, relations)
    source, source_state, target, target_state, relations, grads = out
    return (
        source[None, None],
        source_state[None],
        target[None, None],
        target_state[None],
        relations,
        grads,
    )


def solution(mesh):
    in_specs = (
        P("blk", "grp", None, None),
        P("blk", "grp", None),
        P("blk", "grp", None, None),
        P("blk", "grp", None),
        P(None, "blk", "grp", None),
        P(None, "blk", "grp"),
        P(),
    )
    out_specs = (
        P("blk", "grp", None, None),
        P("blk", "grp", None),
        P("blk", "grp", None, None),
        P("blk", "grp", None),
        P(),
        P(),
    )
    return jax.shard_map(shards, mesh=mesh, in_specs=in_specs, out_specs=out_specs, check_vma=False)
```

```python
import functools
import math

import jax
import jax.numpy as jnp
from jax import lax
from jax.experimental import pallas as pl
from jax.experimental.pallas import tpu as pltpu
from jax.sharding import PartitionSpec as P

entity_rate = 0.1
operator_rate = 0.01
grad_gain = 6.0

f32, bf16 = jnp.float32, jnp.bfloat16
MESH = pl.DeviceIdType.MESH

W = 400
S = 768
D = 512
C = 256
STEPS = 4
NX, NY, NZ = 4, 4, 8
MAIN, TAIL, TILES = 150, 8, 320
PART = 100
HALF, P1, P2, P3 = TILES // 2, TILES // 8, TILES // 32, 2
N_EX, N_1, N_2, N_3, N_4, N_5, N_6, N_7, N_ALL = 0, 2, 5, 8, 15, 22, 25, 28, 32
RING_ORDER = (2, 1, 3)
Z_ORDER = (4, 3, 5, 2, 6, 1, 7)


def dot(a, b, ca, cb):
    return lax.dot_general(a, b, (((ca,), (cb,)), ((), ())), preferred_element_type=f32)


def split(v):
    high = v.astype(bf16)
    return high, (v - high.astype(f32)).astype(bf16)


def dot3(ah, al, bh, bl, ca, cb):
    return dot(ah, bh, ca, cb) + (dot(ah, bl, ca, cb) + dot(al, bh, ca, cb))


def dot3_rows(ah, al, bh, bl):
    left = jnp.concatenate([ah, ah, al], axis=0)
    right = jnp.concatenate([bh, bl, bh], axis=0)
    return dot(left, right, 0, 0)


def adagrad(values, state, gradient):
    state_new = state + jnp.sum(gradient * gradient, axis=0, keepdims=True) * (1.0 / W)
    return values - gradient * (entity_rate / jnp.sqrt(state_new)), state_new


def unpack(gall, u, r, store):
    base = r * HALF
    for c in range(3):
        store(c * 128, (c + 1) * 128, gall[u, pl.ds(base + c * 50, 50)].reshape(W, 128))
    rows = []
    for i in range(2):
        t = base + MAIN + i * 4
        rows.append(jnp.concatenate([gall[u, t + c] for c in range(4)], axis=1))
    rows.append(jnp.zeros((112, D), f32))
    store(384, W, jnp.concatenate(rows, axis=0).T[:W, :16])


def kernel(
    gradient_scale,
    x_in,
    xst_in,
    y_in,
    yst_in,
    pos_in,
    rid_in,
    rel_in,
    x,
    xst,
    yin,
    gall,
    y,
    yst,
    pos,
    rid,
    rel,
    ysend,
    xh,
    xl,
    yh,
    yl,
    qh,
    ql,
    sc,
    sh,
    sl,
    gh,
    gl,
    rh,
    rl,
    acc,
    rx,
    r1,
    b1,
    r2,
    b2,
    r3,
    g3,
    g2,
    y_ssem,
    y_rsem,
    ssem,
    rsem,
    lsem,
):
    blk, grp = lax.axis_index("blk"), lax.axis_index("grp")
    core = blk % 2
    my_y = blk // 4
    my_x = (grp % 2) * 2 + (blk // 2) % 2
    my_z = grp // 2
    first = my_x * (1 - core) + my_y * core
    second = my_y * (1 - core) + my_x * core

    def at(px, py, pz, pc):
        return ((py * 2 + px % 2) * 2 + pc, pz * 2 + px // 2)

    def first_peer(p):
        return at(p * (1 - core) + my_x * core, p * core + my_y * (1 - core), my_z, core)

    def second_peer(p):
        return at(p * core + my_x * (1 - core), p * (1 - core) + my_y * core, my_z, core)

    def z_peer(p):
        return at(my_x, my_y, p, core)

    other = at(my_x, my_y, my_z, 1 - core)
    behind = ((blk + 1) % 16, grp)
    far = ((blk + 15 + 2 * core) % 16, grp)

    barrier = pltpu.get_barrier_semaphore()
    peers = [other, far]
    peers += [first_peer((first + j) % 4) for j in range(1, 4)]
    peers += [second_peer((second + j) % 4) for j in range(1, 4)]
    peers += [z_peer((my_z + j) % NZ) for j in range(1, NZ)]
    for peer in peers:
        pl.semaphore_signal(barrier, inc=1, device_id=peer, device_id_type=MESH)

    loads = [
        pltpu.make_async_copy(src, dst, lsem.at[n])
        for n, (src, dst) in enumerate(
            (
                (rel_in, rel),
                (rid_in, rid),
                (x_in, x),
                (y_in, y),
                (yst_in, yst),
                (pos_in, pos),
                (xst_in, xst),
            )
        )
    ]
    for copy in loads:
        copy.start()
    gh[W:] = jnp.zeros((D - W, S), bf16)
    gl[W:] = jnp.zeros((D - W, S), bf16)
    for r in range(2):
        pad = r * HALF + MAIN
        acc[pad : pad + 10] = jnp.zeros((10, 8, 128), f32)
    b2[P2:] = jnp.zeros((P3 * NZ - P2, 8, 128), f32)
    loads[0].wait()
    rh[...], rl[...] = split(rel[...])
    loads[1].wait()
    loads[2].wait()
    xh[...], xl[...] = split(x[...])
    for copy in loads[3:]:
        copy.wait()
    for c in range(2):
        yin[0, c, :W] = y[:, c * C : (c + 1) * C]
        yin[0, c, W:] = jnp.broadcast_to(yst[:, c * C : (c + 1) * C], (8, C))

    def queries(k):
        r = rid[k]
        qh[...], ql[...] = split(dot3_rows(rh[r], rl[r], xh[...], xl[...]))

    def scores(k, arrived):
        for c in range(2):
            if arrived is not None:
                arrived[c].wait_recv()
            high, low = split(yin[k, c, :W])
            yh[:, c * C : (c + 1) * C] = high
            yl[:, c * C : (c + 1) * C] = low
            sc[c * C : (c + 1) * C] = dot3_rows(high, low, qh[...], ql[...])
        for n in range(3):
            part = slice(n * 256, (n + 1) * 256)
            s = sc[:, part]
            e = jnp.exp(s - jnp.max(s, axis=0, keepdims=True))
            chance = e * (1.0 / jnp.sum(e, axis=0, keepdims=True))
            rows = lax.broadcasted_iota(jnp.int32, (D, 256), 0)
            onehot = (rows == pos[k, :, part]).astype(f32)
            sh[:, part], sl[:, part] = split(chance - onehot)

    def new_targets(k, c):
        part = slice(c * C, (c + 1) * C)
        grad = dot3(qh[...], ql[...], sh[part], sl[part], 1, 1)
        rows, state = adagrad(yin[k, c, :W], yin[k, c, W : W + 1], grad)
        ysend[k, c, :W] = rows
        ysend[k, c, W:] = jnp.broadcast_to(state, (8, C))

    def send_targets(k, c):
        copy = pltpu.make_async_remote_copy(
            src_ref=ysend.at[k, c],
            dst_ref=yin.at[k + 1, c],
            send_sem=y_ssem.at[k, c],
            recv_sem=y_rsem.at[k, c],
            device_id=behind,
            device_id_type=MESH,
        )
        copy.start()
        return copy

    def query_grad():
        gh[:W], gl[:W] = split(dot3(yh[...], yl[...], sh[...], sl[...], 1, 0))

    def operator_grad(k, h, add):
        part = slice(h * 256, (h + 1) * 256)
        og = dot3(xh[...], xl[...], gh[part], gl[part], 1, 1)
        for r in range(2):
            mine = rid[k] == r
            for c in range(2 - h):
                to = pl.ds(r * HALF + (2 * h + c) * 50, 50)
                new = jnp.where(mine, og[:, c * 128 : (c + 1) * 128].reshape(50, 8, 128), 0.0)
                acc[to] = acc[to] + new if add else new
        if h == 0:
            return
        tail = og[:, 128:].T[:16]
        for r in range(2):
            mine = rid[k] == r
            for i in range(2):
                for c in range(4):
                    n = 128 if c < 3 else 16
                    t = r * HALF + MAIN + i * 4 + c
                    new = jnp.where(mine, tail[i * 8 : (i + 1) * 8, c * 128 : c * 128 + n], 0.0)
                    acc[t, :, :n] = acc[t, :, :n] + new if add else new

    def new_sources(k):
        r = rid[k]
        grad = dot3(rh[r], rl[r], gh[:W], gl[:W], 1, 0)
        rows, state = adagrad(x[...], xst[...], grad)
        x[...] = rows
        xst[...] = state
        xh[...], xl[...] = split(rows)

    def update(u, _):
        def send(number, src, dst, peer):
            copy = pltpu.make_async_remote_copy(
                src_ref=src,
                dst_ref=dst,
                send_sem=ssem.at[u, number],
                recv_sem=rsem.at[u, number],
                device_id=peer,
                device_id_type=MESH,
            )
            copy.start()
            return copy

        k = 2 * u
        queries(k)
        scores(k, None)
        new_targets(k, 0)

        @pl.when(u == 0)
        def _():
            pl.semaphore_wait(barrier, len(peers))

        moved = [send_targets(k, 0)]
        new_targets(k, 1)
        moved.append(send_targets(k, 1))
        query_grad()
        for h in range(2):
            operator_grad(k, h, False)
        new_sources(k)
        queries(k + 1)
        scores(k + 1, moved)
        query_grad()

        sent = []
        for h in range(2):
            operator_grad(k + 1, h, True)
            start, size = (0, PART) if h == 0 else (PART, HALF - PART)
            theirs = pl.ds((1 - core) * HALF + start, size)
            sent.append(send(N_EX + h, acc.at[theirs], rx.at[u, pl.ds(start, size)], other))
        new_sources(k + 1)

        for copy in sent:
            copy.wait_recv()

        def chip_sum(p):
            r1[pl.ds(p * P1, P1)] = acc[pl.ds(core * HALF + p * P1, P1)] + rx[u, pl.ds(p * P1, P1)]

        got = []
        for j in RING_ORDER:
            p = (first + j) % 4
            chip_sum(p)
            got.append(send(N_1 + j - 1, r1.at[pl.ds(p * P1, P1)], b1.at[u, j - 1], first_peer(p)))
        chip_sum(first)
        sent += got
        for c in range(2):
            new_targets(k + 1, c)
        for copy in got:
            copy.wait_recv()
        r2[...] = r1[pl.ds(first * P1, P1)] + b1[u, 0] + b1[u, 1] + b1[u, 2]
        got = []
        for j in RING_ORDER:
            p = (second + j) % 4
            got.append(send(N_2 + j - 1, r2.at[pl.ds(p * P2, P2)], r3.at[u, j - 1], second_peer(p)))
        sent += got
        moved2 = [send_targets(k + 1, c) for c in range(2)]
        for copy in got:
            copy.wait_recv()
        b2[:P2] = r2[pl.ds(second * P2, P2)] + r3[u, 0] + r3[u, 1] + r3[u, 2]
        got = []
        for j in Z_ORDER:
            p = (my_z + j) % NZ
            got.append(send(N_3 + j - 1, b2.at[pl.ds(p * P3, P3)], g3.at[u, j], z_peer(p)))
        sent += got
        for copy in got:
            copy.wait_recv()
        total = b2[pl.ds(my_z * P3, P3)]
        for j in range(1, NZ):
            total = total + g3[u, j]
        g3[u, 0] = gradient_scale * total
        mine = pl.ds(my_z * P3, P3)
        g2[u, mine] = g3[u, 0]
        got = []
        for j in Z_ORDER:
            p = (my_z + j) % NZ
            got.append(send(N_4 + j - 1, g3.at[u, 0], g2.at[u, mine], z_peer(p)))
        sent += got
        for copy in got:
            copy.wait_recv()
        mine = pl.ds((core * 4 + first) * P1 + second * P2, P2)
        gall[u, mine] = g2[u, pl.ds(0, P2)]
        got = []
        for j in RING_ORDER:
            p = (second + j) % 4
            got.append(send(N_5 + j - 1, g2.at[u, pl.ds(0, P2)], gall.at[u, mine], second_peer(p)))
        sent += got
        for copy in got:
            copy.wait_recv()
        mine = pl.ds((core * 4 + first) * P1, P1)
        got = []
        for j in RING_ORDER:
            p = (first + j) % 4
            got.append(send(N_6 + j - 1, gall.at[u, mine], gall.at[u, mine], first_peer(p)))
        sent += got
        across = [send(N_7, gall.at[u, mine], gall.at[u, mine], other)]
        for n, j in ((1, 1), (2, 3), (0, 2)):
            got[n].wait_recv()
            theirs = pl.ds((core * 4 + (first + 4 - j) % 4) * P1, P1)
            across.append(send(N_7 + j, gall.at[u, theirs], gall.at[u, theirs], other))
        sent += across

        def apply(r):
            def store(start, end, values):
                rel[r, :, start:end] = rel[r, :, start:end] - operator_rate * values

            @pl.when(u == 0)
            def _():
                unpack(gall, u, r, store)
                rh[r], rl[r] = split(rel[r])

        apply(core)
        for copy in across:
            copy.wait_recv()
        apply(1 - core)
        for copy in moved + moved2 + sent:
            copy.wait_send()
        for copy in moved2:
            copy.wait_recv()
        return 0

    lax.fori_loop(0, STEPS // 2, update, 0)


def finish(x, xst, yin, gall, rel, x_out, xst_out, y_out, yst_out, rel_out, og_out, og, rel_new, sem):
    copies = [pltpu.make_async_copy(x, x_out, sem.at[0])]
    for c in range(2):
        part = pl.ds(c * C, C)
        rows = yin.at[STEPS, c, pl.ds(0, W)]
        copies.append(pltpu.make_async_copy(rows, y_out.at[:, part], sem.at[1 + c]))
    for copy in copies:
        copy.start()
    xst_out[...] = xst[...]
    for c in range(2):
        yst_out[:, c * C : (c + 1) * C] = yin[STEPS, c, W : W + 1]
    for r in range(2):
        for u in range(2):

            def store(start, end, values):
                og[u, r, :, start:end] = values
                before = rel[r, :, start:end] if u == 0 else rel_new[r, :, start:end]
                rel_new[r, :, start:end] = before - operator_rate * values

            unpack(gall, u, r, store)
            copies.append(pltpu.make_async_copy(og.at[u, r], og_out.at[u, r], sem.at[3 + 2 * u + r]))
            copies[-1].start()
        copies.append(pltpu.make_async_copy(rel_new.at[r], rel_out.at[r], sem.at[7 + r]))
        copies[-1].start()
    for copy in copies:
        copy.wait()


def shards(
    source_rows, source_state, target_rows, destination_state, positives, relation_ids, relations
):
    everyone = S * lax.axis_size("blk") * lax.axis_size("grp")
    gradient_scale = grad_gain / math.sqrt(everyone)
    vmem = pl.BlockSpec(memory_space=pltpu.VMEM)
    hbm = pl.BlockSpec(memory_space=pltpu.HBM)
    tiles = (8, 128)
    operands = (
        source_rows[0, 0],
        source_state[0],
        target_rows[0, 0],
        destination_state[0],
        positives[:, 0],
        relation_ids[:, 0, 0],
        relations,
    )
    source, source_state, target, grads = pl.pallas_call(
        functools.partial(kernel, gradient_scale),
        out_shape=(
            jax.ShapeDtypeStruct((W, S), f32),
            jax.ShapeDtypeStruct((1, S), f32),
            jax.ShapeDtypeStruct((STEPS + 1, 2, W + 8, C), f32),
            jax.ShapeDtypeStruct((2, TILES, *tiles), f32),
        ),
        in_specs=[hbm] * 7,
        out_specs=(vmem,) * 4,
        scratch_shapes=[
            pltpu.VMEM((W, D), f32),
            pltpu.VMEM((1, D), f32),
            pltpu.VMEM((STEPS, 1, S), jnp.int32),
            pltpu.SMEM((STEPS,), jnp.int32),
            pltpu.VMEM((2, W, W), f32),
            pltpu.VMEM((STEPS, 2, W + 8, C), f32),
            pltpu.VMEM((W, S), bf16),
            pltpu.VMEM((W, S), bf16),
            pltpu.VMEM((W, D), bf16),
            pltpu.VMEM((W, D), bf16),
            pltpu.VMEM((W, S), bf16),
            pltpu.VMEM((W, S), bf16),
            pltpu.VMEM((D, S), f32),
            pltpu.VMEM((D, S), bf16),
            pltpu.VMEM((D, S), bf16),
            pltpu.VMEM((D, S), bf16),
            pltpu.VMEM((D, S), bf16),
            pltpu.VMEM((2, W, W), bf16),
            pltpu.VMEM((2, W, W), bf16),
            pltpu.VMEM((TILES, *tiles), f32),
            pltpu.VMEM((2, HALF, *tiles), f32),
            pltpu.VMEM((HALF, *tiles), f32),
            pltpu.VMEM((2, 3, P1, *tiles), f32),
            pltpu.VMEM((P1, *tiles), f32),
            pltpu.VMEM((P3 * NZ, *tiles), f32),
            pltpu.VMEM((2, 3, P2, *tiles), f32),
            pltpu.VMEM((2, NZ, P3, *tiles), f32),
            pltpu.VMEM((2, P3 * NZ, *tiles), f32),
            pltpu.SemaphoreType.DMA((STEPS, 2)),
            pltpu.SemaphoreType.DMA((STEPS, 2)),
            pltpu.SemaphoreType.DMA((2, N_ALL)),
            pltpu.SemaphoreType.DMA((2, N_ALL)),
            pltpu.SemaphoreType.DMA((7,)),
        ],
        compiler_params=pltpu.CompilerParams(
            collective_id=0, has_side_effects=True, vmem_limit_bytes=36 << 20
        ),
        name="train",
    )(*(pltpu.with_memory_space_constraint(operand, pltpu.HBM) for operand in operands))
    out = pl.pallas_call(
        finish,
        out_shape=(
            jax.ShapeDtypeStruct((W, S), f32),
            jax.ShapeDtypeStruct((1, S), f32),
            jax.ShapeDtypeStruct((W, D), f32),
            jax.ShapeDtypeStruct((1, D), f32),
            jax.ShapeDtypeStruct((2, W, W), f32),
            jax.ShapeDtypeStruct((2, 2, W, W), f32),
        ),
        in_specs=[vmem] * 5,
        out_specs=(hbm, vmem, hbm, vmem, hbm, hbm),
        scratch_shapes=[
            pltpu.VMEM((2, 2, W, W), f32),
            pltpu.VMEM((2, W, W), f32),
            pltpu.SemaphoreType.DMA((9,)),
        ],
        compiler_params=pltpu.CompilerParams(vmem_limit_bytes=24 << 20),
        name="finish",
    )(source, source_state, target, grads, relations)
    source, source_state, target, target_state, relations, grads = out
    return (
        source[None, None],
        source_state[None],
        target[None, None],
        target_state[None],
        relations,
        grads,
    )


def solution(mesh):
    in_specs = (
        P("blk", "grp", None, None),
        P("blk", "grp", None),
        P("blk", "grp", None, None),
        P("blk", "grp", None),
        P(None, "blk", "grp", None),
        P(None, "blk", "grp"),
        P(),
    )
    out_specs = (
        P("blk", "grp", None, None),
        P("blk", "grp", None),
        P("blk", "grp", None, None),
        P("blk", "grp", None),
        P(),
        P(),
    )
    return jax.shard_map(shards, mesh=mesh, in_specs=in_specs, out_specs=out_specs, check_vma=False)
```

```python
import functools
import math

import jax
import jax.numpy as jnp
from jax import lax
from jax.experimental import pallas as pl
from jax.experimental.pallas import tpu as pltpu
from jax.sharding import PartitionSpec as P

entity_rate = 0.1
operator_rate = 0.01
grad_gain = 6.0

f32, bf16 = jnp.float32, jnp.bfloat16
MESH = pl.DeviceIdType.MESH

W = 400
S = 768
D = 512
C = 256
STEPS = 4
NX, NY, NZ = 4, 4, 8
MAIN, TAIL, TILES = 150, 8, 320
PART = 100
HALF, P1, P2, P3 = TILES // 2, TILES // 8, TILES // 32, 2
N_EX, N_1, N_2, N_3, N_4, N_5, N_6, N_7, N_ALL = 0, 2, 14, 17, 24, 31, 34, 46, 62
RING_ORDER = (2, 1, 3)
ARRIVAL = (1, 3, 2)
Z_ORDER = (4, 3, 5, 2, 6, 1, 7)


def dot(a, b, ca, cb):
    return lax.dot_general(a, b, (((ca,), (cb,)), ((), ())), preferred_element_type=f32)


def split(v):
    high = v.astype(bf16)
    return high, (v - high.astype(f32)).astype(bf16)


def dot3(ah, al, bh, bl, ca, cb):
    return dot(ah, bh, ca, cb) + (dot(ah, bl, ca, cb) + dot(al, bh, ca, cb))


def dot3_rows(ah, al, bh, bl):
    left = jnp.concatenate([ah, ah, al], axis=0)
    right = jnp.concatenate([bh, bl, bh], axis=0)
    return dot(left, right, 0, 0)


def adagrad(values, state, gradient):
    state_new = state + jnp.sum(gradient * gradient, axis=0, keepdims=True) * (1.0 / W)
    return values - gradient * (entity_rate / jnp.sqrt(state_new)), state_new


def unpack(gall, u, r, store):
    base = r * HALF
    for c in range(3):
        store(c * 128, (c + 1) * 128, gall[u, pl.ds(base + c * 50, 50)].reshape(W, 128))
    rows = []
    for i in range(2):
        t = base + MAIN + i * 4
        rows.append(jnp.concatenate([gall[u, t + c] for c in range(4)], axis=1))
    rows.append(jnp.zeros((112, D), f32))
    store(384, W, jnp.concatenate(rows, axis=0).T[:W, :16])


def kernel(
    gradient_scale,
    x_in,
    xst_in,
    y_in,
    yst_in,
    pos_in,
    rid_in,
    rel_in,
    x,
    xst,
    yin,
    gall,
    y,
    yst,
    pos,
    rid,
    rel,
    ysend,
    xh,
    xl,
    yh,
    yl,
    qh,
    ql,
    sc,
    sh,
    sl,
    gh,
    gl,
    rh,
    rl,
    acc,
    rx,
    r1,
    b1,
    r2,
    b2,
    r3,
    g3,
    g2,
    y_ssem,
    y_rsem,
    ssem,
    rsem,
    lsem,
):
    blk, grp = lax.axis_index("blk"), lax.axis_index("grp")
    core = blk % 2
    my_y = blk // 4
    my_x = (grp % 2) * 2 + (blk // 2) % 2
    my_z = grp // 2
    first = my_x * (1 - core) + my_y * core
    second = my_y * (1 - core) + my_x * core

    def at(px, py, pz, pc):
        return ((py * 2 + px % 2) * 2 + pc, pz * 2 + px // 2)

    def first_peer(p):
        return at(p * (1 - core) + my_x * core, p * core + my_y * (1 - core), my_z, core)

    def second_peer(p):
        return at(p * core + my_x * (1 - core), p * (1 - core) + my_y * core, my_z, core)

    def z_peer(p):
        return at(my_x, my_y, p, core)

    other = at(my_x, my_y, my_z, 1 - core)
    behind = ((blk + 1) % 16, grp)
    far = ((blk + 15 + 2 * core) % 16, grp)

    barrier = pltpu.get_barrier_semaphore()
    peers = [other, far]
    peers += [first_peer((first + j) % 4) for j in range(1, 4)]
    peers += [second_peer((second + j) % 4) for j in range(1, 4)]
    peers += [z_peer((my_z + j) % NZ) for j in range(1, NZ)]
    for peer in peers:
        pl.semaphore_signal(barrier, inc=1, device_id=peer, device_id_type=MESH)

    loads = [
        pltpu.make_async_copy(src, dst, lsem.at[n])
        for n, (src, dst) in enumerate(
            (
                (rel_in, rel),
                (rid_in, rid),
                (x_in, x),
                (y_in, y),
                (yst_in, yst),
                (pos_in, pos),
                (xst_in, xst),
            )
        )
    ]
    for copy in loads:
        copy.start()
    gh[W:] = jnp.zeros((D - W, S), bf16)
    gl[W:] = jnp.zeros((D - W, S), bf16)
    for r in range(2):
        pad = r * HALF + MAIN
        acc[pad : pad + 10] = jnp.zeros((10, 8, 128), f32)
    b2[P2:] = jnp.zeros((P3 * NZ - P2, 8, 128), f32)
    loads[0].wait()
    rh[...], rl[...] = split(rel[...])
    loads[1].wait()
    loads[2].wait()
    xh[...], xl[...] = split(x[...])
    for copy in loads[3:]:
        copy.wait()
    for c in range(2):
        yin[0, c, :W] = y[:, c * C : (c + 1) * C]
        yin[0, c, W:] = jnp.broadcast_to(yst[:, c * C : (c + 1) * C], (8, C))

    def queries(k):
        r = rid[k]
        qh[...], ql[...] = split(dot3_rows(rh[r], rl[r], xh[...], xl[...]))

    def scores(k, arrived):
        for c in range(2):
            if arrived is not None:
                arrived[c].wait_recv()
            high, low = split(yin[k, c, :W])
            yh[:, c * C : (c + 1) * C] = high
            yl[:, c * C : (c + 1) * C] = low
            sc[c * C : (c + 1) * C] = dot3_rows(high, low, qh[...], ql[...])
        for n in range(3):
            part = slice(n * 256, (n + 1) * 256)
            s = sc[:, part]
            e = jnp.exp(s - jnp.max(s, axis=0, keepdims=True))
            chance = e * (1.0 / jnp.sum(e, axis=0, keepdims=True))
            rows = lax.broadcasted_iota(jnp.int32, (D, 256), 0)
            onehot = (rows == pos[k, :, part]).astype(f32)
            sh[:, part], sl[:, part] = split(chance - onehot)

    def new_targets(k, c):
        part = slice(c * C, (c + 1) * C)
        grad = dot3(qh[...], ql[...], sh[part], sl[part], 1, 1)
        rows, state = adagrad(yin[k, c, :W], yin[k, c, W : W + 1], grad)
        ysend[k, c, :W] = rows
        ysend[k, c, W:] = jnp.broadcast_to(state, (8, C))

    def send_targets(k, c):
        copy = pltpu.make_async_remote_copy(
            src_ref=ysend.at[k, c],
            dst_ref=yin.at[k + 1, c],
            send_sem=y_ssem.at[k, c],
            recv_sem=y_rsem.at[k, c],
            device_id=behind,
            device_id_type=MESH,
        )
        copy.start()
        return copy

    def query_grad():
        gh[:W], gl[:W] = split(dot3(yh[...], yl[...], sh[...], sl[...], 1, 0))

    def operator_grad(k, h, add):
        part = slice(h * 256, (h + 1) * 256)
        og = dot3(xh[...], xl[...], gh[part], gl[part], 1, 1)
        for r in range(2):
            mine = rid[k] == r
            for c in range(2 - h):
                to = pl.ds(r * HALF + (2 * h + c) * 50, 50)
                new = jnp.where(mine, og[:, c * 128 : (c + 1) * 128].reshape(50, 8, 128), 0.0)
                acc[to] = acc[to] + new if add else new
        if h == 0:
            return
        tail = og[:, 128:].T[:16]
        for r in range(2):
            mine = rid[k] == r
            for i in range(2):
                for c in range(4):
                    n = 128 if c < 3 else 16
                    t = r * HALF + MAIN + i * 4 + c
                    new = jnp.where(mine, tail[i * 8 : (i + 1) * 8, c * 128 : c * 128 + n], 0.0)
                    acc[t, :, :n] = acc[t, :, :n] + new if add else new

    def new_sources(k):
        r = rid[k]
        grad = dot3(rh[r], rl[r], gh[:W], gl[:W], 1, 0)
        rows, state = adagrad(x[...], xst[...], grad)
        x[...] = rows
        xst[...] = state
        xh[...], xl[...] = split(rows)

    def update(u, _):
        def send(number, src, dst, peer):
            copy = pltpu.make_async_remote_copy(
                src_ref=src,
                dst_ref=dst,
                send_sem=ssem.at[u, number],
                recv_sem=rsem.at[u, number],
                device_id=peer,
                device_id_type=MESH,
            )
            copy.start()
            return copy

        k = 2 * u
        queries(k)
        scores(k, None)
        new_targets(k, 0)

        @pl.when(u == 0)
        def _():
            pl.semaphore_wait(barrier, len(peers))

        moved = [send_targets(k, 0)]
        new_targets(k, 1)
        moved.append(send_targets(k, 1))
        query_grad()
        for h in range(2):
            operator_grad(k, h, False)
        new_sources(k)
        queries(k + 1)
        scores(k + 1, moved)
        query_grad()

        sent = []
        for h in range(2):
            operator_grad(k + 1, h, True)
            start, size = (0, PART) if h == 0 else (PART, HALF - PART)
            theirs = pl.ds((1 - core) * HALF + start, size)
            sent.append(send(N_EX + h, acc.at[theirs], rx.at[u, pl.ds(start, size)], other))
        new_sources(k + 1)

        for copy in sent:
            copy.wait_recv()

        def chip_sum(p):
            r1[pl.ds(p * P1, P1)] = acc[pl.ds(core * HALF + p * P1, P1)] + rx[u, pl.ds(p * P1, P1)]

        for p in range(4):
            chip_sum(p)
        got = {}
        for t in (*RING_ORDER, 0):
            q = (second + t) % 4
            for j in RING_ORDER:
                p = (first + j) % 4
                src = r1.at[pl.ds(p * P1 + q * P2, P2)]
                n = 4 * (j - 1) + t
                got[j, t] = send(N_1 + n, src, b1.at[u, n], first_peer(p))
        sent += got.values()
        for c in range(2):
            new_targets(k + 1, c)

        def ring_sum(t):
            for j in ARRIVAL:
                got[j, t].wait_recv()
            own = r1[pl.ds(first * P1 + (second + t) % 4 * P2, P2)]
            return own + b1[u, t] + b1[u, 4 + t] + b1[u, 8 + t]

        got2 = []
        for t in RING_ORDER:
            r2[t] = ring_sum(t)
            got2.append(send(N_2 + t - 1, r2.at[t], r3.at[u, t - 1], second_peer((second + t) % 4)))
        sent += got2
        total = ring_sum(0)
        for copy in got2:
            copy.wait_recv()
        b2[:P2] = total + r3[u, 0] + r3[u, 1] + r3[u, 2]
        got = []
        for j in Z_ORDER:
            p = (my_z + j) % NZ
            got.append(send(N_3 + j - 1, b2.at[pl.ds(p * P3, P3)], g3.at[u, j], z_peer(p)))
        sent += got
        moved2 = [send_targets(k + 1, c) for c in range(2)]
        for copy in got:
            copy.wait_recv()
        total = b2[pl.ds(my_z * P3, P3)]
        for j in range(1, NZ):
            total = total + g3[u, j]
        g3[u, 0] = gradient_scale * total
        mine = pl.ds(my_z * P3, P3)
        g2[u, mine] = g3[u, 0]
        got = []
        for j in Z_ORDER:
            p = (my_z + j) % NZ
            got.append(send(N_4 + j - 1, g3.at[u, 0], g2.at[u, mine], z_peer(p)))
        sent += got
        for copy in got:
            copy.wait_recv()
        def place(f, s_):
            return pl.ds((core * 4 + f) * P1 + s_ * P2, P2)

        across, around = [], {}

        def cross(n, where):
            across.append(send(N_7 + n, gall.at[u, where], gall.at[u, where], other))

        def spread(t, where):
            for j in RING_ORDER:
                n = 4 * (j - 1) + t
                peer = first_peer((first + j) % 4)
                around[j, t] = send(N_6 + n, gall.at[u, where], gall.at[u, where], peer)

        mine = place(first, second)
        gall[u, mine] = g2[u, pl.ds(0, P2)]
        got2 = {}
        for j in RING_ORDER:
            peer = second_peer((second + j) % 4)
            got2[j] = send(N_5 + j - 1, gall.at[u, mine], gall.at[u, mine], peer)
        spread(0, mine)
        cross(0, mine)
        for t in ARRIVAL:
            got2[t].wait_recv()
            theirs = place(first, (second + 4 - t) % 4)
            spread(t, theirs)
            cross(t, theirs)
        for t in (0, *ARRIVAL):
            for j in ARRIVAL:
                around[j, t].wait_recv()
                cross(4 * j + t, place((first + 4 - j) % 4, (second + 4 - t) % 4))
        sent += [*got2.values(), *around.values(), *across]

        def apply(r):
            def store(start, end, values):
                rel[r, :, start:end] = rel[r, :, start:end] - operator_rate * values

            @pl.when(u == 0)
            def _():
                unpack(gall, u, r, store)
                rh[r], rl[r] = split(rel[r])

        apply(core)
        for copy in across:
            copy.wait_recv()
        apply(1 - core)
        for copy in moved + moved2 + sent:
            copy.wait_send()
        for copy in moved2:
            copy.wait_recv()
        return 0

    lax.fori_loop(0, STEPS // 2, update, 0)


def finish(x, xst, yin, gall, rel, x_out, xst_out, y_out, yst_out, rel_out, og_out, og, rel_new, sem):
    copies = [pltpu.make_async_copy(x, x_out, sem.at[0])]
    for c in range(2):
        part = pl.ds(c * C, C)
        rows = yin.at[STEPS, c, pl.ds(0, W)]
        copies.append(pltpu.make_async_copy(rows, y_out.at[:, part], sem.at[1 + c]))
    for copy in copies:
        copy.start()
    xst_out[...] = xst[...]
    for c in range(2):
        yst_out[:, c * C : (c + 1) * C] = yin[STEPS, c, W : W + 1]
    for r in range(2):
        for u in range(2):

            def store(start, end, values):
                og[u, r, :, start:end] = values
                before = rel[r, :, start:end] if u == 0 else rel_new[r, :, start:end]
                rel_new[r, :, start:end] = before - operator_rate * values

            unpack(gall, u, r, store)
            copies.append(pltpu.make_async_copy(og.at[u, r], og_out.at[u, r], sem.at[3 + 2 * u + r]))
            copies[-1].start()
        copies.append(pltpu.make_async_copy(rel_new.at[r], rel_out.at[r], sem.at[7 + r]))
        copies[-1].start()
    for copy in copies:
        copy.wait()


def shards(
    source_rows, source_state, target_rows, destination_state, positives, relation_ids, relations
):
    everyone = S * lax.axis_size("blk") * lax.axis_size("grp")
    gradient_scale = grad_gain / math.sqrt(everyone)
    vmem = pl.BlockSpec(memory_space=pltpu.VMEM)
    hbm = pl.BlockSpec(memory_space=pltpu.HBM)
    tiles = (8, 128)
    operands = (
        source_rows[0, 0],
        source_state[0],
        target_rows[0, 0],
        destination_state[0],
        positives[:, 0],
        relation_ids[:, 0, 0],
        relations,
    )
    source, source_state, target, grads = pl.pallas_call(
        functools.partial(kernel, gradient_scale),
        out_shape=(
            jax.ShapeDtypeStruct((W, S), f32),
            jax.ShapeDtypeStruct((1, S), f32),
            jax.ShapeDtypeStruct((STEPS + 1, 2, W + 8, C), f32),
            jax.ShapeDtypeStruct((2, TILES, *tiles), f32),
        ),
        in_specs=[hbm] * 7,
        out_specs=(vmem,) * 4,
        scratch_shapes=[
            pltpu.VMEM((W, D), f32),
            pltpu.VMEM((1, D), f32),
            pltpu.VMEM((STEPS, 1, S), jnp.int32),
            pltpu.SMEM((STEPS,), jnp.int32),
            pltpu.VMEM((2, W, W), f32),
            pltpu.VMEM((STEPS, 2, W + 8, C), f32),
            pltpu.VMEM((W, S), bf16),
            pltpu.VMEM((W, S), bf16),
            pltpu.VMEM((W, D), bf16),
            pltpu.VMEM((W, D), bf16),
            pltpu.VMEM((W, S), bf16),
            pltpu.VMEM((W, S), bf16),
            pltpu.VMEM((D, S), f32),
            pltpu.VMEM((D, S), bf16),
            pltpu.VMEM((D, S), bf16),
            pltpu.VMEM((D, S), bf16),
            pltpu.VMEM((D, S), bf16),
            pltpu.VMEM((2, W, W), bf16),
            pltpu.VMEM((2, W, W), bf16),
            pltpu.VMEM((TILES, *tiles), f32),
            pltpu.VMEM((2, HALF, *tiles), f32),
            pltpu.VMEM((HALF, *tiles), f32),
            pltpu.VMEM((2, 12, P2, *tiles), f32),
            pltpu.VMEM((4, P2, *tiles), f32),
            pltpu.VMEM((P3 * NZ, *tiles), f32),
            pltpu.VMEM((2, 3, P2, *tiles), f32),
            pltpu.VMEM((2, NZ, P3, *tiles), f32),
            pltpu.VMEM((2, P3 * NZ, *tiles), f32),
            pltpu.SemaphoreType.DMA((STEPS, 2)),
            pltpu.SemaphoreType.DMA((STEPS, 2)),
            pltpu.SemaphoreType.DMA((2, N_ALL)),
            pltpu.SemaphoreType.DMA((2, N_ALL)),
            pltpu.SemaphoreType.DMA((7,)),
        ],
        compiler_params=pltpu.CompilerParams(
            collective_id=0, has_side_effects=True, vmem_limit_bytes=36 << 20
        ),
        name="train",
    )(*(pltpu.with_memory_space_constraint(operand, pltpu.HBM) for operand in operands))
    out = pl.pallas_call(
        finish,
        out_shape=(
            jax.ShapeDtypeStruct((W, S), f32),
            jax.ShapeDtypeStruct((1, S), f32),
            jax.ShapeDtypeStruct((W, D), f32),
            jax.ShapeDtypeStruct((1, D), f32),
            jax.ShapeDtypeStruct((2, W, W), f32),
            jax.ShapeDtypeStruct((2, 2, W, W), f32),
        ),
        in_specs=[vmem] * 5,
        out_specs=(hbm, vmem, hbm, vmem, hbm, hbm),
        scratch_shapes=[
            pltpu.VMEM((2, 2, W, W), f32),
            pltpu.VMEM((2, W, W), f32),
            pltpu.SemaphoreType.DMA((9,)),
        ],
        compiler_params=pltpu.CompilerParams(vmem_limit_bytes=24 << 20),
        name="finish",
    )(source, source_state, target, grads, relations)
    source, source_state, target, target_state, relations, grads = out
    return (
        source[None, None],
        source_state[None],
        target[None, None],
        target_state[None],
        relations,
        grads,
    )


def solution(mesh):
    in_specs = (
        P("blk", "grp", None, None),
        P("blk", "grp", None),
        P("blk", "grp", None, None),
        P("blk", "grp", None),
        P(None, "blk", "grp", None),
        P(None, "blk", "grp"),
        P(),
    )
    out_specs = (
        P("blk", "grp", None, None),
        P("blk", "grp", None),
        P("blk", "grp", None, None),
        P("blk", "grp", None),
        P(),
        P(),
    )
    return jax.shard_map(shards, mesh=mesh, in_specs=in_specs, out_specs=out_specs, check_vma=False)
```

```python
import functools
import math

import jax
import jax.numpy as jnp
from jax import lax
from jax.experimental import pallas as pl
from jax.experimental.pallas import tpu as pltpu
from jax.sharding import PartitionSpec as P

entity_rate = 0.1
operator_rate = 0.01
grad_gain = 6.0

f32, bf16 = jnp.float32, jnp.bfloat16
MESH = pl.DeviceIdType.MESH

W = 400
S = 768
D = 512
C = 256
STEPS = 4
NX, NY, NZ = 4, 4, 8
MAIN, TAIL, TILES = 150, 8, 320
PART = 100
HALF, P1, P2, P3 = TILES // 2, TILES // 8, TILES // 32, 2
N_EX, N_1, N_2, N_3, N_4, N_5, N_6, N_7, N_ALL = 0, 2, 14, 17, 24, 31, 34, 46, 62
RING_ORDER = (2, 1, 3)
ARRIVAL = (1, 3, 2)
Z_ORDER = (4, 3, 5, 2, 6, 1, 7)


def dot(a, b, ca, cb):
    return lax.dot_general(a, b, (((ca,), (cb,)), ((), ())), preferred_element_type=f32)


def split(v):
    high = v.astype(bf16)
    return high, (v - high.astype(f32)).astype(bf16)


def dot3(ah, al, bh, bl, ca, cb):
    return dot(ah, bh, ca, cb) + (dot(ah, bl, ca, cb) + dot(al, bh, ca, cb))


def dot3_rows(ah, al, bh, bl):
    left = jnp.concatenate([ah, ah, al], axis=0)
    right = jnp.concatenate([bh, bl, bh], axis=0)
    return dot(left, right, 0, 0)


def adagrad(values, state, gradient):
    state_new = state + jnp.sum(gradient * gradient, axis=0, keepdims=True) * (1.0 / W)
    return values - gradient * (entity_rate / jnp.sqrt(state_new)), state_new


def unpack(gall, u, r, store):
    base = r * HALF
    for c in range(3):
        store(c * 128, (c + 1) * 128, gall[u, pl.ds(base + c * 50, 50)].reshape(W, 128))
    rows = []
    for i in range(2):
        t = base + MAIN + i * 4
        rows.append(jnp.concatenate([gall[u, t + c] for c in range(4)], axis=1))
    rows.append(jnp.zeros((112, D), f32))
    store(384, W, jnp.concatenate(rows, axis=0).T[:W, :16])


def kernel(
    gradient_scale,
    x_in,
    xst_in,
    y_in,
    yst_in,
    pos_in,
    rid_in,
    rel_in,
    x,
    xst,
    yin,
    gall,
    y,
    yst,
    pos,
    rid,
    rel,
    ysend,
    xh,
    xl,
    yh,
    yl,
    qh,
    ql,
    sc,
    sh,
    sl,
    gh,
    gl,
    rh,
    rl,
    acc,
    rx,
    r1,
    b1,
    r2,
    b2,
    r3,
    g3,
    g2,
    y_ssem,
    y_rsem,
    ssem,
    rsem,
    lsem,
):
    blk, grp = lax.axis_index("blk"), lax.axis_index("grp")
    core = blk % 2
    my_y = blk // 4
    my_x = (grp % 2) * 2 + (blk // 2) % 2
    my_z = grp // 2
    first = my_x * (1 - core) + my_y * core
    second = my_y * (1 - core) + my_x * core

    def at(px, py, pz, pc):
        return ((py * 2 + px % 2) * 2 + pc, pz * 2 + px // 2)

    def first_peer(p):
        return at(p * (1 - core) + my_x * core, p * core + my_y * (1 - core), my_z, core)

    def second_peer(p):
        return at(p * core + my_x * (1 - core), p * (1 - core) + my_y * core, my_z, core)

    def z_peer(p):
        return at(my_x, my_y, p, core)

    other = at(my_x, my_y, my_z, 1 - core)
    behind = ((blk + 1) % 16, grp)
    far = ((blk + 15 + 2 * core) % 16, grp)

    barrier = pltpu.get_barrier_semaphore()
    peers = [other, far]
    peers += [first_peer((first + j) % 4) for j in range(1, 4)]
    peers += [second_peer((second + j) % 4) for j in range(1, 4)]
    peers += [z_peer((my_z + j) % NZ) for j in range(1, NZ)]
    for peer in peers:
        pl.semaphore_signal(barrier, inc=1, device_id=peer, device_id_type=MESH)

    loads = [
        pltpu.make_async_copy(src, dst, lsem.at[n])
        for n, (src, dst) in enumerate(
            (
                (rel_in, rel),
                (rid_in, rid),
                (x_in, x),
                (y_in, y),
                (yst_in, yst),
                (pos_in, pos),
                (xst_in, xst),
            )
        )
    ]
    for copy in loads:
        copy.start()
    gh[W:] = jnp.zeros((D - W, S), bf16)
    gl[W:] = jnp.zeros((D - W, S), bf16)
    for r in range(2):
        pad = r * HALF + MAIN
        acc[pad : pad + 10] = jnp.zeros((10, 8, 128), f32)
    b2[P2:] = jnp.zeros((P3 * NZ - P2, 8, 128), f32)
    loads[0].wait()
    rh[...], rl[...] = split(rel[...])
    loads[1].wait()
    loads[2].wait()
    xh[...], xl[...] = split(x[...])
    for copy in loads[3:]:
        copy.wait()
    for c in range(2):
        yin[0, c, :W] = y[:, c * C : (c + 1) * C]
        yin[0, c, W:] = jnp.broadcast_to(yst[:, c * C : (c + 1) * C], (8, C))

    def queries(k):
        r = rid[k]
        qh[...], ql[...] = split(dot3_rows(rh[r], rl[r], xh[...], xl[...]))

    def scores(k, arrived):
        for c in range(2):
            if arrived is not None:
                arrived[c].wait_recv()
            high, low = split(yin[k, c, :W])
            yh[:, c * C : (c + 1) * C] = high
            yl[:, c * C : (c + 1) * C] = low
            sc[c * C : (c + 1) * C] = dot3_rows(high, low, qh[...], ql[...])
        for n in range(3):
            part = slice(n * 256, (n + 1) * 256)
            s = sc[:, part]
            e = jnp.exp(s - jnp.max(s, axis=0, keepdims=True))
            chance = e * (1.0 / jnp.sum(e, axis=0, keepdims=True))
            rows = lax.broadcasted_iota(jnp.int32, (D, 256), 0)
            onehot = (rows == pos[k, :, part]).astype(f32)
            sh[:, part], sl[:, part] = split(chance - onehot)

    def new_targets(k, c):
        part = slice(c * C, (c + 1) * C)
        grad = dot3(qh[...], ql[...], sh[part], sl[part], 1, 1)
        rows, state = adagrad(yin[k, c, :W], yin[k, c, W : W + 1], grad)
        ysend[k, c, :W] = rows
        ysend[k, c, W:] = jnp.broadcast_to(state, (8, C))

    def send_targets(k, c):
        copy = pltpu.make_async_remote_copy(
            src_ref=ysend.at[k, c],
            dst_ref=yin.at[k + 1, c],
            send_sem=y_ssem.at[k, c],
            recv_sem=y_rsem.at[k, c],
            device_id=behind,
            device_id_type=MESH,
        )
        copy.start()
        return copy

    def query_grad():
        gh[:W], gl[:W] = split(dot3(yh[...], yl[...], sh[...], sl[...], 1, 0))

    def operator_grad(k, h, add):
        part = slice(h * 256, (h + 1) * 256)
        og = dot3(xh[...], xl[...], gh[part], gl[part], 1, 1)
        for r in range(2):
            mine = rid[k] == r
            for c in range(2 - h):
                to = pl.ds(r * HALF + (2 * h + c) * 50, 50)
                new = jnp.where(mine, og[:, c * 128 : (c + 1) * 128].reshape(50, 8, 128), 0.0)
                acc[to] = acc[to] + new if add else new
        if h == 0:
            return
        tail = og[:, 128:].T[:16]
        for r in range(2):
            mine = rid[k] == r
            for i in range(2):
                for c in range(4):
                    n = 128 if c < 3 else 16
                    t = r * HALF + MAIN + i * 4 + c
                    new = jnp.where(mine, tail[i * 8 : (i + 1) * 8, c * 128 : c * 128 + n], 0.0)
                    acc[t, :, :n] = acc[t, :, :n] + new if add else new

    def new_sources(k):
        r = rid[k]
        grad = dot3(rh[r], rl[r], gh[:W], gl[:W], 1, 0)
        rows, state = adagrad(x[...], xst[...], grad)
        x[...] = rows
        xst[...] = state
        xh[...], xl[...] = split(rows)

    def update(u, _):
        def send(number, src, dst, peer):
            copy = pltpu.make_async_remote_copy(
                src_ref=src,
                dst_ref=dst,
                send_sem=ssem.at[u, number],
                recv_sem=rsem.at[u, number],
                device_id=peer,
                device_id_type=MESH,
            )
            copy.start()
            return copy

        k = 2 * u
        queries(k)
        scores(k, None)
        new_targets(k, 0)

        @pl.when(u == 0)
        def _():
            pl.semaphore_wait(barrier, len(peers))

        moved = [send_targets(k, 0)]
        new_targets(k, 1)
        moved.append(send_targets(k, 1))
        query_grad()
        for h in range(2):
            operator_grad(k, h, False)
        new_sources(k)
        queries(k + 1)
        scores(k + 1, moved)
        moved2 = []
        for c in range(2):
            new_targets(k + 1, c)
            moved2.append(send_targets(k + 1, c))
        query_grad()

        sent = []
        for h in range(2):
            operator_grad(k + 1, h, True)
            start, size = (0, PART) if h == 0 else (PART, HALF - PART)
            theirs = pl.ds((1 - core) * HALF + start, size)
            sent.append(send(N_EX + h, acc.at[theirs], rx.at[u, pl.ds(start, size)], other))
        new_sources(k + 1)

        for copy in sent:
            copy.wait_recv()

        def chip_sum(p):
            r1[pl.ds(p * P1, P1)] = acc[pl.ds(core * HALF + p * P1, P1)] + rx[u, pl.ds(p * P1, P1)]

        for p in range(4):
            chip_sum(p)
        got = {}
        for t in (*RING_ORDER, 0):
            q = (second + t) % 4
            for j in RING_ORDER:
                p = (first + j) % 4
                src = r1.at[pl.ds(p * P1 + q * P2, P2)]
                n = 4 * (j - 1) + t
                got[j, t] = send(N_1 + n, src, b1.at[u, n], first_peer(p))
        sent += got.values()
        def ring_sum(t):
            for j in ARRIVAL:
                got[j, t].wait_recv()
            own = r1[pl.ds(first * P1 + (second + t) % 4 * P2, P2)]
            return own + b1[u, t] + b1[u, 4 + t] + b1[u, 8 + t]

        got2 = []
        for t in RING_ORDER:
            r2[t] = ring_sum(t)
            got2.append(send(N_2 + t - 1, r2.at[t], r3.at[u, t - 1], second_peer((second + t) % 4)))
        sent += got2
        total = ring_sum(0)
        for copy in got2:
            copy.wait_recv()
        b2[:P2] = total + r3[u, 0] + r3[u, 1] + r3[u, 2]
        got = []
        for j in Z_ORDER:
            p = (my_z + j) % NZ
            got.append(send(N_3 + j - 1, b2.at[pl.ds(p * P3, P3)], g3.at[u, j], z_peer(p)))
        sent += got
        for copy in got:
            copy.wait_recv()
        total = b2[pl.ds(my_z * P3, P3)]
        for j in range(1, NZ):
            total = total + g3[u, j]
        g3[u, 0] = gradient_scale * total
        mine = pl.ds(my_z * P3, P3)
        g2[u, mine] = g3[u, 0]
        got = []
        for j in Z_ORDER:
            p = (my_z + j) % NZ
            got.append(send(N_4 + j - 1, g3.at[u, 0], g2.at[u, mine], z_peer(p)))
        sent += got
        for copy in got:
            copy.wait_recv()
        def place(f, s_):
            return pl.ds((core * 4 + f) * P1 + s_ * P2, P2)

        across, around = [], {}

        def cross(n, where):
            across.append(send(N_7 + n, gall.at[u, where], gall.at[u, where], other))

        def spread(t, where):
            for j in RING_ORDER:
                n = 4 * (j - 1) + t
                peer = first_peer((first + j) % 4)
                around[j, t] = send(N_6 + n, gall.at[u, where], gall.at[u, where], peer)

        mine = place(first, second)
        gall[u, mine] = g2[u, pl.ds(0, P2)]
        got2 = {}
        for j in RING_ORDER:
            peer = second_peer((second + j) % 4)
            got2[j] = send(N_5 + j - 1, gall.at[u, mine], gall.at[u, mine], peer)
        spread(0, mine)
        cross(0, mine)
        for t in ARRIVAL:
            got2[t].wait_recv()
            theirs = place(first, (second + 4 - t) % 4)
            spread(t, theirs)
            cross(t, theirs)
        for t in (0, *ARRIVAL):
            for j in ARRIVAL:
                around[j, t].wait_recv()
                cross(4 * j + t, place((first + 4 - j) % 4, (second + 4 - t) % 4))
        sent += [*got2.values(), *around.values(), *across]

        def apply(r):
            def store(start, end, values):
                rel[r, :, start:end] = rel[r, :, start:end] - operator_rate * values

            @pl.when(u == 0)
            def _():
                unpack(gall, u, r, store)
                rh[r], rl[r] = split(rel[r])

        apply(core)
        for copy in across:
            copy.wait_recv()
        apply(1 - core)
        for copy in moved + moved2 + sent:
            copy.wait_send()
        for copy in moved2:
            copy.wait_recv()
        return 0

    lax.fori_loop(0, STEPS // 2, update, 0)


def finish(x, xst, yin, gall, rel, x_out, xst_out, y_out, yst_out, rel_out, og_out, og, rel_new, sem):
    copies = [pltpu.make_async_copy(x, x_out, sem.at[0])]
    for c in range(2):
        part = pl.ds(c * C, C)
        rows = yin.at[STEPS, c, pl.ds(0, W)]
        copies.append(pltpu.make_async_copy(rows, y_out.at[:, part], sem.at[1 + c]))
    for copy in copies:
        copy.start()
    xst_out[...] = xst[...]
    for c in range(2):
        yst_out[:, c * C : (c + 1) * C] = yin[STEPS, c, W : W + 1]
    for r in range(2):
        for u in range(2):

            def store(start, end, values):
                og[u, r, :, start:end] = values
                before = rel[r, :, start:end] if u == 0 else rel_new[r, :, start:end]
                rel_new[r, :, start:end] = before - operator_rate * values

            unpack(gall, u, r, store)
            copies.append(pltpu.make_async_copy(og.at[u, r], og_out.at[u, r], sem.at[3 + 2 * u + r]))
            copies[-1].start()
        copies.append(pltpu.make_async_copy(rel_new.at[r], rel_out.at[r], sem.at[7 + r]))
        copies[-1].start()
    for copy in copies:
        copy.wait()


def shards(
    source_rows, source_state, target_rows, destination_state, positives, relation_ids, relations
):
    everyone = S * lax.axis_size("blk") * lax.axis_size("grp")
    gradient_scale = grad_gain / math.sqrt(everyone)
    vmem = pl.BlockSpec(memory_space=pltpu.VMEM)
    hbm = pl.BlockSpec(memory_space=pltpu.HBM)
    tiles = (8, 128)
    operands = (
        source_rows[0, 0],
        source_state[0],
        target_rows[0, 0],
        destination_state[0],
        positives[:, 0],
        relation_ids[:, 0, 0],
        relations,
    )
    source, source_state, target, grads = pl.pallas_call(
        functools.partial(kernel, gradient_scale),
        out_shape=(
            jax.ShapeDtypeStruct((W, S), f32),
            jax.ShapeDtypeStruct((1, S), f32),
            jax.ShapeDtypeStruct((STEPS + 1, 2, W + 8, C), f32),
            jax.ShapeDtypeStruct((2, TILES, *tiles), f32),
        ),
        in_specs=[hbm] * 7,
        out_specs=(vmem,) * 4,
        scratch_shapes=[
            pltpu.VMEM((W, D), f32),
            pltpu.VMEM((1, D), f32),
            pltpu.VMEM((STEPS, 1, S), jnp.int32),
            pltpu.SMEM((STEPS,), jnp.int32),
            pltpu.VMEM((2, W, W), f32),
            pltpu.VMEM((STEPS, 2, W + 8, C), f32),
            pltpu.VMEM((W, S), bf16),
            pltpu.VMEM((W, S), bf16),
            pltpu.VMEM((W, D), bf16),
            pltpu.VMEM((W, D), bf16),
            pltpu.VMEM((W, S), bf16),
            pltpu.VMEM((W, S), bf16),
            pltpu.VMEM((D, S), f32),
            pltpu.VMEM((D, S), bf16),
            pltpu.VMEM((D, S), bf16),
            pltpu.VMEM((D, S), bf16),
            pltpu.VMEM((D, S), bf16),
            pltpu.VMEM((2, W, W), bf16),
            pltpu.VMEM((2, W, W), bf16),
            pltpu.VMEM((TILES, *tiles), f32),
            pltpu.VMEM((2, HALF, *tiles), f32),
            pltpu.VMEM((HALF, *tiles), f32),
            pltpu.VMEM((2, 12, P2, *tiles), f32),
            pltpu.VMEM((4, P2, *tiles), f32),
            pltpu.VMEM((P3 * NZ, *tiles), f32),
            pltpu.VMEM((2, 3, P2, *tiles), f32),
            pltpu.VMEM((2, NZ, P3, *tiles), f32),
            pltpu.VMEM((2, P3 * NZ, *tiles), f32),
            pltpu.SemaphoreType.DMA((STEPS, 2)),
            pltpu.SemaphoreType.DMA((STEPS, 2)),
            pltpu.SemaphoreType.DMA((2, N_ALL)),
            pltpu.SemaphoreType.DMA((2, N_ALL)),
            pltpu.SemaphoreType.DMA((7,)),
        ],
        compiler_params=pltpu.CompilerParams(
            collective_id=0, has_side_effects=True, vmem_limit_bytes=36 << 20
        ),
        name="train",
    )(*(pltpu.with_memory_space_constraint(operand, pltpu.HBM) for operand in operands))
    out = pl.pallas_call(
        finish,
        out_shape=(
            jax.ShapeDtypeStruct((W, S), f32),
            jax.ShapeDtypeStruct((1, S), f32),
            jax.ShapeDtypeStruct((W, D), f32),
            jax.ShapeDtypeStruct((1, D), f32),
            jax.ShapeDtypeStruct((2, W, W), f32),
            jax.ShapeDtypeStruct((2, 2, W, W), f32),
        ),
        in_specs=[vmem] * 5,
        out_specs=(hbm, vmem, hbm, vmem, hbm, hbm),
        scratch_shapes=[
            pltpu.VMEM((2, 2, W, W), f32),
            pltpu.VMEM((2, W, W), f32),
            pltpu.SemaphoreType.DMA((9,)),
        ],
        compiler_params=pltpu.CompilerParams(vmem_limit_bytes=24 << 20),
        name="finish",
    )(source, source_state, target, grads, relations)
    source, source_state, target, target_state, relations, grads = out
    return (
        source[None, None],
        source_state[None],
        target[None, None],
        target_state[None],
        relations,
        grads,
    )


def solution(mesh):
    in_specs = (
        P("blk", "grp", None, None),
        P("blk", "grp", None),
        P("blk", "grp", None, None),
        P("blk", "grp", None),
        P(None, "blk", "grp", None),
        P(None, "blk", "grp"),
        P(),
    )
    out_specs = (
        P("blk", "grp", None, None),
        P("blk", "grp", None),
        P("blk", "grp", None, None),
        P("blk", "grp", None),
        P(),
        P(),
    )
    return jax.shard_map(shards, mesh=mesh, in_specs=in_specs, out_specs=out_specs, check_vma=False)
```

```python
import functools
import math

import jax
import jax.numpy as jnp
from jax import lax
from jax.experimental import pallas as pl
from jax.experimental.pallas import tpu as pltpu
from jax.sharding import PartitionSpec as P

entity_rate = 0.1
operator_rate = 0.01
grad_gain = 6.0

f32, bf16 = jnp.float32, jnp.bfloat16
MESH = pl.DeviceIdType.MESH

W = 400
S = 768
D = 512
C = 256
STEPS = 4
NX, NY, NZ = 4, 4, 8
MAIN, TAIL, TILES = 150, 8, 320
PART = 100
HALF, P1, P2, P3 = TILES // 2, TILES // 8, TILES // 32, 2
N_EX, N_1, N_2, N_3, N_4, N_5, N_6, N_7, N_ALL = 0, 2, 14, 17, 24, 31, 34, 46, 62
RING_ORDER = (2, 1, 3)
ARRIVAL = (1, 3, 2)
Z_ORDER = (4, 3, 5, 2, 6, 1, 7)


def dot(a, b, ca, cb):
    return lax.dot_general(a, b, (((ca,), (cb,)), ((), ())), preferred_element_type=f32)


def split(v):
    high = v.astype(bf16)
    return high, (v - high.astype(f32)).astype(bf16)


def dot3(ah, al, bh, bl, ca, cb):
    return dot(ah, bh, ca, cb) + (dot(ah, bl, ca, cb) + dot(al, bh, ca, cb))


def dot3_rows(ah, al, bh, bl):
    left = jnp.concatenate([ah, ah, al], axis=0)
    right = jnp.concatenate([bh, bl, bh], axis=0)
    return dot(left, right, 0, 0)


def adagrad(values, state, gradient):
    state_new = state + jnp.sum(gradient * gradient, axis=0, keepdims=True) * (1.0 / W)
    return values - gradient * (entity_rate / jnp.sqrt(state_new)), state_new


def unpack(gall, u, r, store):
    base = r * HALF
    for c in range(3):
        store(c * 128, (c + 1) * 128, gall[u, pl.ds(base + c * 50, 50)].reshape(W, 128))
    rows = []
    for i in range(2):
        t = base + MAIN + i * 4
        rows.append(jnp.concatenate([gall[u, t + c] for c in range(4)], axis=1))
    rows.append(jnp.zeros((112, D), f32))
    store(384, W, jnp.concatenate(rows, axis=0).T[:W, :16])


def kernel(
    gradient_scale,
    x_in,
    xst_in,
    y_in,
    yst_in,
    pos_in,
    rid_in,
    rel_in,
    x,
    xst,
    yin,
    gall,
    y,
    yst,
    pos,
    rid,
    rel,
    ysend,
    xh,
    xl,
    yh,
    yl,
    qh,
    ql,
    sc,
    sh,
    sl,
    gh,
    gl,
    rh,
    rl,
    acc,
    rx,
    r1,
    b1,
    r2,
    b2,
    r3,
    g3,
    g2,
    y_ssem,
    y_rsem,
    ssem,
    rsem,
    lsem,
):
    blk, grp = lax.axis_index("blk"), lax.axis_index("grp")
    core = blk % 2
    my_y = blk // 4
    my_x = (grp % 2) * 2 + (blk // 2) % 2
    my_z = grp // 2
    first = my_x * (1 - core) + my_y * core
    second = my_y * (1 - core) + my_x * core

    def at(px, py, pz, pc):
        return ((py * 2 + px % 2) * 2 + pc, pz * 2 + px // 2)

    def first_peer(p):
        return at(p * (1 - core) + my_x * core, p * core + my_y * (1 - core), my_z, core)

    def second_peer(p):
        return at(p * core + my_x * (1 - core), p * (1 - core) + my_y * core, my_z, core)

    def z_peer(p):
        return at(my_x, my_y, p, core)

    other = at(my_x, my_y, my_z, 1 - core)
    behind = ((blk + 1) % 16, grp)
    far = ((blk + 15 + 2 * core) % 16, grp)

    barrier = pltpu.get_barrier_semaphore()
    peers = [other, far]
    peers += [first_peer((first + j) % 4) for j in range(1, 4)]
    peers += [second_peer((second + j) % 4) for j in range(1, 4)]
    peers += [z_peer((my_z + j) % NZ) for j in range(1, NZ)]
    for peer in peers:
        pl.semaphore_signal(barrier, inc=1, device_id=peer, device_id_type=MESH)

    loads = [
        pltpu.make_async_copy(src, dst, lsem.at[n])
        for n, (src, dst) in enumerate(
            (
                (rel_in, rel),
                (rid_in, rid),
                (x_in, x),
                (y_in, y),
                (yst_in, yst),
                (pos_in, pos),
                (xst_in, xst),
            )
        )
    ]
    for copy in loads:
        copy.start()
    gh[W:] = jnp.zeros((D - W, S), bf16)
    gl[W:] = jnp.zeros((D - W, S), bf16)
    for r in range(2):
        pad = r * HALF + MAIN
        acc[pad : pad + 10] = jnp.zeros((10, 8, 128), f32)
    b2[P2:] = jnp.zeros((P3 * NZ - P2, 8, 128), f32)
    loads[0].wait()
    rh[...], rl[...] = split(rel[...])
    loads[1].wait()
    loads[2].wait()
    xh[...], xl[...] = split(x[...])
    for copy in loads[3:]:
        copy.wait()
    for c in range(2):
        yin[0, c, :W] = y[:, c * C : (c + 1) * C]
        yin[0, c, W:] = jnp.broadcast_to(yst[:, c * C : (c + 1) * C], (8, C))

    def queries(k):
        r = rid[k]
        qh[...], ql[...] = split(dot3_rows(rh[r], rl[r], xh[...], xl[...]))

    def scores(k, arrived):
        for c in range(2):
            if arrived is not None:
                arrived[c].wait_recv()
            high, low = split(yin[k, c, :W])
            yh[:, c * C : (c + 1) * C] = high
            yl[:, c * C : (c + 1) * C] = low
            sc[c * C : (c + 1) * C] = dot3_rows(high, low, qh[...], ql[...])
        for n in range(3):
            part = slice(n * 256, (n + 1) * 256)
            s = sc[:, part]
            e = jnp.exp(s - jnp.max(s, axis=0, keepdims=True))
            chance = e * (1.0 / jnp.sum(e, axis=0, keepdims=True))
            rows = lax.broadcasted_iota(jnp.int32, (D, 256), 0)
            onehot = (rows == pos[k, :, part]).astype(f32)
            sh[:, part], sl[:, part] = split(chance - onehot)

    def new_targets(k, c):
        part = slice(c * C, (c + 1) * C)
        grad = dot3(qh[...], ql[...], sh[part], sl[part], 1, 1)
        rows, state = adagrad(yin[k, c, :W], yin[k, c, W : W + 1], grad)
        ysend[k, c, :W] = rows
        ysend[k, c, W:] = jnp.broadcast_to(state, (8, C))

    def target_copy(k, c):
        return pltpu.make_async_remote_copy(
            src_ref=ysend.at[k, c],
            dst_ref=yin.at[k + 1, c],
            send_sem=y_ssem.at[k, c],
            recv_sem=y_rsem.at[k, c],
            device_id=behind,
            device_id_type=MESH,
        )

    def send_targets(k, c):
        copy = target_copy(k, c)
        copy.start()
        return copy

    def query_grad():
        gh[:W], gl[:W] = split(dot3(yh[...], yl[...], sh[...], sl[...], 1, 0))

    def operator_grad(k, h, add):
        part = slice(h * 256, (h + 1) * 256)
        og = dot3(xh[...], xl[...], gh[part], gl[part], 1, 1)
        for r in range(2):
            mine = rid[k] == r
            for c in range(2 - h):
                to = pl.ds(r * HALF + (2 * h + c) * 50, 50)
                new = jnp.where(mine, og[:, c * 128 : (c + 1) * 128].reshape(50, 8, 128), 0.0)
                acc[to] = acc[to] + new if add else new
        if h == 0:
            return
        tail = og[:, 128:].T[:16]
        for r in range(2):
            mine = rid[k] == r
            for i in range(2):
                for c in range(4):
                    n = 128 if c < 3 else 16
                    t = r * HALF + MAIN + i * 4 + c
                    new = jnp.where(mine, tail[i * 8 : (i + 1) * 8, c * 128 : c * 128 + n], 0.0)
                    acc[t, :, :n] = acc[t, :, :n] + new if add else new

    def new_sources(k):
        r = rid[k]
        grad = dot3(rh[r], rl[r], gh[:W], gl[:W], 1, 0)
        rows, state = adagrad(x[...], xst[...], grad)
        x[...] = rows
        xst[...] = state
        xh[...], xl[...] = split(rows)

    def update(u, _):
        def send(number, src, dst, peer):
            copy = pltpu.make_async_remote_copy(
                src_ref=src,
                dst_ref=dst,
                send_sem=ssem.at[u, number],
                recv_sem=rsem.at[u, number],
                device_id=peer,
                device_id_type=MESH,
            )
            copy.start()
            return copy

        k = 2 * u
        queries(k)
        scores(k, None)
        new_targets(k, 0)

        @pl.when(u == 0)
        def _():
            pl.semaphore_wait(barrier, len(peers))

        moved = [send_targets(k, 0)]
        new_targets(k, 1)
        moved.append(send_targets(k, 1))
        query_grad()
        for h in range(2):
            operator_grad(k, h, False)
        new_sources(k)
        queries(k + 1)
        scores(k + 1, moved)

        def targets_of(which):
            @pl.when(core == which)
            def _():
                for c in range(2):
                    new_targets(k + 1, c)
                    send_targets(k + 1, c)

        targets_of(1)
        moved2 = [target_copy(k + 1, c) for c in range(2)]
        query_grad()

        sent = []
        for h in range(2):
            operator_grad(k + 1, h, True)
            start, size = (0, PART) if h == 0 else (PART, HALF - PART)
            theirs = pl.ds((1 - core) * HALF + start, size)
            sent.append(send(N_EX + h, acc.at[theirs], rx.at[u, pl.ds(start, size)], other))
        for copy in sent:
            copy.wait_recv()

        def chip_sum(p):
            r1[pl.ds(p * P1, P1)] = acc[pl.ds(core * HALF + p * P1, P1)] + rx[u, pl.ds(p * P1, P1)]

        for p in range(4):
            chip_sum(p)
        got = {}
        for t in (*RING_ORDER, 0):
            q = (second + t) % 4
            for j in RING_ORDER:
                p = (first + j) % 4
                src = r1.at[pl.ds(p * P1 + q * P2, P2)]
                n = 4 * (j - 1) + t
                got[j, t] = send(N_1 + n, src, b1.at[u, n], first_peer(p))
        sent += got.values()
        targets_of(0)
        new_sources(k + 1)

        def ring_sum(t):
            for j in ARRIVAL:
                got[j, t].wait_recv()
            own = r1[pl.ds(first * P1 + (second + t) % 4 * P2, P2)]
            return own + b1[u, t] + b1[u, 4 + t] + b1[u, 8 + t]

        got2 = []
        for t in RING_ORDER:
            r2[t] = ring_sum(t)
            got2.append(send(N_2 + t - 1, r2.at[t], r3.at[u, t - 1], second_peer((second + t) % 4)))
        sent += got2
        total = ring_sum(0)
        for copy in got2:
            copy.wait_recv()
        b2[:P2] = total + r3[u, 0] + r3[u, 1] + r3[u, 2]
        got = []
        for j in Z_ORDER:
            p = (my_z + j) % NZ
            got.append(send(N_3 + j - 1, b2.at[pl.ds(p * P3, P3)], g3.at[u, j], z_peer(p)))
        sent += got
        for copy in got:
            copy.wait_recv()
        total = b2[pl.ds(my_z * P3, P3)]
        for j in range(1, NZ):
            total = total + g3[u, j]
        g3[u, 0] = gradient_scale * total
        mine = pl.ds(my_z * P3, P3)
        g2[u, mine] = g3[u, 0]
        got = []
        for j in Z_ORDER:
            p = (my_z + j) % NZ
            got.append(send(N_4 + j - 1, g3.at[u, 0], g2.at[u, mine], z_peer(p)))
        sent += got
        for copy in got:
            copy.wait_recv()
        def place(f, s_):
            return pl.ds((core * 4 + f) * P1 + s_ * P2, P2)

        across, around = [], {}

        def cross(n, where):
            across.append(send(N_7 + n, gall.at[u, where], gall.at[u, where], other))

        def spread(t, where):
            for j in RING_ORDER:
                n = 4 * (j - 1) + t
                peer = first_peer((first + j) % 4)
                around[j, t] = send(N_6 + n, gall.at[u, where], gall.at[u, where], peer)

        mine = place(first, second)
        gall[u, mine] = g2[u, pl.ds(0, P2)]
        got2 = {}
        for j in RING_ORDER:
            peer = second_peer((second + j) % 4)
            got2[j] = send(N_5 + j - 1, gall.at[u, mine], gall.at[u, mine], peer)
        spread(0, mine)
        cross(0, mine)
        for t in ARRIVAL:
            got2[t].wait_recv()
            theirs = place(first, (second + 4 - t) % 4)
            spread(t, theirs)
            cross(t, theirs)
        for t in (0, *ARRIVAL):
            for j in ARRIVAL:
                around[j, t].wait_recv()
                cross(4 * j + t, place((first + 4 - j) % 4, (second + 4 - t) % 4))
        sent += [*got2.values(), *around.values(), *across]

        def apply(r):
            def store(start, end, values):
                rel[r, :, start:end] = rel[r, :, start:end] - operator_rate * values

            @pl.when(u == 0)
            def _():
                unpack(gall, u, r, store)
                rh[r], rl[r] = split(rel[r])

        apply(core)
        for copy in across:
            copy.wait_recv()
        apply(1 - core)
        for copy in moved + moved2 + sent:
            copy.wait_send()
        for copy in moved2:
            copy.wait_recv()
        return 0

    lax.fori_loop(0, STEPS // 2, update, 0)


def finish(x, xst, yin, gall, rel, x_out, xst_out, y_out, yst_out, rel_out, og_out, og, rel_new, sem):
    copies = [pltpu.make_async_copy(x, x_out, sem.at[0])]
    for c in range(2):
        part = pl.ds(c * C, C)
        rows = yin.at[STEPS, c, pl.ds(0, W)]
        copies.append(pltpu.make_async_copy(rows, y_out.at[:, part], sem.at[1 + c]))
    for copy in copies:
        copy.start()
    xst_out[...] = xst[...]
    for c in range(2):
        yst_out[:, c * C : (c + 1) * C] = yin[STEPS, c, W : W + 1]
    for r in range(2):
        for u in range(2):

            def store(start, end, values):
                og[u, r, :, start:end] = values
                before = rel[r, :, start:end] if u == 0 else rel_new[r, :, start:end]
                rel_new[r, :, start:end] = before - operator_rate * values

            unpack(gall, u, r, store)
            copies.append(pltpu.make_async_copy(og.at[u, r], og_out.at[u, r], sem.at[3 + 2 * u + r]))
            copies[-1].start()
        copies.append(pltpu.make_async_copy(rel_new.at[r], rel_out.at[r], sem.at[7 + r]))
        copies[-1].start()
    for copy in copies:
        copy.wait()


def shards(
    source_rows, source_state, target_rows, destination_state, positives, relation_ids, relations
):
    everyone = S * lax.axis_size("blk") * lax.axis_size("grp")
    gradient_scale = grad_gain / math.sqrt(everyone)
    vmem = pl.BlockSpec(memory_space=pltpu.VMEM)
    hbm = pl.BlockSpec(memory_space=pltpu.HBM)
    tiles = (8, 128)
    operands = (
        source_rows[0, 0],
        source_state[0],
        target_rows[0, 0],
        destination_state[0],
        positives[:, 0],
        relation_ids[:, 0, 0],
        relations,
    )
    source, source_state, target, grads = pl.pallas_call(
        functools.partial(kernel, gradient_scale),
        out_shape=(
            jax.ShapeDtypeStruct((W, S), f32),
            jax.ShapeDtypeStruct((1, S), f32),
            jax.ShapeDtypeStruct((STEPS + 1, 2, W + 8, C), f32),
            jax.ShapeDtypeStruct((2, TILES, *tiles), f32),
        ),
        in_specs=[hbm] * 7,
        out_specs=(vmem,) * 4,
        scratch_shapes=[
            pltpu.VMEM((W, D), f32),
            pltpu.VMEM((1, D), f32),
            pltpu.VMEM((STEPS, 1, S), jnp.int32),
            pltpu.SMEM((STEPS,), jnp.int32),
            pltpu.VMEM((2, W, W), f32),
            pltpu.VMEM((STEPS, 2, W + 8, C), f32),
            pltpu.VMEM((W, S), bf16),
            pltpu.VMEM((W, S), bf16),
            pltpu.VMEM((W, D), bf16),
            pltpu.VMEM((W, D), bf16),
            pltpu.VMEM((W, S), bf16),
            pltpu.VMEM((W, S), bf16),
            pltpu.VMEM((D, S), f32),
            pltpu.VMEM((D, S), bf16),
            pltpu.VMEM((D, S), bf16),
            pltpu.VMEM((D, S), bf16),
            pltpu.VMEM((D, S), bf16),
            pltpu.VMEM((2, W, W), bf16),
            pltpu.VMEM((2, W, W), bf16),
            pltpu.VMEM((TILES, *tiles), f32),
            pltpu.VMEM((2, HALF, *tiles), f32),
            pltpu.VMEM((HALF, *tiles), f32),
            pltpu.VMEM((2, 12, P2, *tiles), f32),
            pltpu.VMEM((4, P2, *tiles), f32),
            pltpu.VMEM((P3 * NZ, *tiles), f32),
            pltpu.VMEM((2, 3, P2, *tiles), f32),
            pltpu.VMEM((2, NZ, P3, *tiles), f32),
            pltpu.VMEM((2, P3 * NZ, *tiles), f32),
            pltpu.SemaphoreType.DMA((STEPS, 2)),
            pltpu.SemaphoreType.DMA((STEPS, 2)),
            pltpu.SemaphoreType.DMA((2, N_ALL)),
            pltpu.SemaphoreType.DMA((2, N_ALL)),
            pltpu.SemaphoreType.DMA((7,)),
        ],
        compiler_params=pltpu.CompilerParams(
            collective_id=0, has_side_effects=True, vmem_limit_bytes=36 << 20
        ),
        name="train",
    )(*(pltpu.with_memory_space_constraint(operand, pltpu.HBM) for operand in operands))
    out = pl.pallas_call(
        finish,
        out_shape=(
            jax.ShapeDtypeStruct((W, S), f32),
            jax.ShapeDtypeStruct((1, S), f32),
            jax.ShapeDtypeStruct((W, D), f32),
            jax.ShapeDtypeStruct((1, D), f32),
            jax.ShapeDtypeStruct((2, W, W), f32),
            jax.ShapeDtypeStruct((2, 2, W, W), f32),
        ),
        in_specs=[vmem] * 5,
        out_specs=(hbm, vmem, hbm, vmem, hbm, hbm),
        scratch_shapes=[
            pltpu.VMEM((2, 2, W, W), f32),
            pltpu.VMEM((2, W, W), f32),
            pltpu.SemaphoreType.DMA((9,)),
        ],
        compiler_params=pltpu.CompilerParams(vmem_limit_bytes=24 << 20),
        name="finish",
    )(source, source_state, target, grads, relations)
    source, source_state, target, target_state, relations, grads = out
    return (
        source[None, None],
        source_state[None],
        target[None, None],
        target_state[None],
        relations,
        grads,
    )


def solution(mesh):
    in_specs = (
        P("blk", "grp", None, None),
        P("blk", "grp", None),
        P("blk", "grp", None, None),
        P("blk", "grp", None),
        P(None, "blk", "grp", None),
        P(None, "blk", "grp"),
        P(),
    )
    out_specs = (
        P("blk", "grp", None, None),
        P("blk", "grp", None),
        P("blk", "grp", None, None),
        P("blk", "grp", None),
        P(),
        P(),
    )
    return jax.shard_map(shards, mesh=mesh, in_specs=in_specs, out_specs=out_specs, check_vma=False)
```

```python
import functools
import math

import jax
import jax.numpy as jnp
from jax import lax
from jax.experimental import pallas as pl
from jax.experimental.pallas import tpu as pltpu
from jax.sharding import PartitionSpec as P

entity_rate = 0.1
operator_rate = 0.01
grad_gain = 6.0

f32, bf16 = jnp.float32, jnp.bfloat16
MESH = pl.DeviceIdType.MESH

W = 400
S = 768
D = 512
C = 256
STEPS = 4
NX, NY, NZ = 4, 4, 8
MAIN, TAIL, TILES = 150, 8, 320
PART = 100
HALF, P1, P2, P3 = TILES // 2, TILES // 8, TILES // 32, 2
N_EX, N_1, N_2, N_3, N_4, N_5, N_6, N_7, N_ALL = 0, 2, 14, 17, 24, 31, 34, 46, 62
RING_ORDER = (2, 1, 3)
ARRIVAL = (1, 3, 2)
Z_ORDER = (4, 3, 5, 2, 6, 1, 7)


def dot(a, b, ca, cb):
    return lax.dot_general(a, b, (((ca,), (cb,)), ((), ())), preferred_element_type=f32)


def split(v):
    high = v.astype(bf16)
    return high, (v - high.astype(f32)).astype(bf16)


def dot3(ah, al, bh, bl, ca, cb):
    return dot(ah, bh, ca, cb) + (dot(ah, bl, ca, cb) + dot(al, bh, ca, cb))


def dot3_rows(ah, al, bh, bl):
    left = jnp.concatenate([ah, ah, al], axis=0)
    right = jnp.concatenate([bh, bl, bh], axis=0)
    return dot(left, right, 0, 0)


def adagrad(values, state, gradient):
    state_new = state + jnp.sum(gradient * gradient, axis=0, keepdims=True) * (1.0 / W)
    return values - gradient * (entity_rate / jnp.sqrt(state_new)), state_new


def unpack(gall, u, r, store):
    base = r * HALF
    for c in range(3):
        store(c * 128, (c + 1) * 128, gall[u, pl.ds(base + c * 50, 50)].reshape(W, 128))
    rows = []
    for i in range(2):
        t = base + MAIN + i * 4
        rows.append(jnp.concatenate([gall[u, t + c] for c in range(4)], axis=1))
    rows.append(jnp.zeros((112, D), f32))
    store(384, W, jnp.concatenate(rows, axis=0).T[:W, :16])


def kernel(
    gradient_scale,
    x_in,
    xst_in,
    y_in,
    yst_in,
    pos_in,
    rid_in,
    rel_in,
    x,
    xst,
    yin,
    gall,
    y,
    yst,
    pos,
    rid,
    rel,
    ysend,
    xh,
    xl,
    yh,
    yl,
    qh,
    ql,
    sc,
    sh,
    sl,
    gh,
    gl,
    rh,
    rl,
    acc,
    rx,
    r1,
    b1,
    r2,
    b2,
    r3,
    g3,
    g2,
    y_ssem,
    y_rsem,
    ssem,
    rsem,
    lsem,
):
    blk, grp = lax.axis_index("blk"), lax.axis_index("grp")
    core = blk % 2
    my_y = blk // 4
    my_x = (grp % 2) * 2 + (blk // 2) % 2
    my_z = grp // 2
    first = my_x * (1 - core) + my_y * core
    second = my_y * (1 - core) + my_x * core

    def at(px, py, pz, pc):
        return ((py * 2 + px % 2) * 2 + pc, pz * 2 + px // 2)

    def first_peer(p):
        return at(p * (1 - core) + my_x * core, p * core + my_y * (1 - core), my_z, core)

    def second_peer(p):
        return at(p * core + my_x * (1 - core), p * (1 - core) + my_y * core, my_z, core)

    def z_peer(p):
        return at(my_x, my_y, p, core)

    other = at(my_x, my_y, my_z, 1 - core)
    behind = ((blk + 1) % 16, grp)
    far = ((blk + 15 + 2 * core) % 16, grp)

    barrier = pltpu.get_barrier_semaphore()
    peers = [other, far]
    peers += [first_peer((first + j) % 4) for j in range(1, 4)]
    peers += [second_peer((second + j) % 4) for j in range(1, 4)]
    peers += [z_peer((my_z + j) % NZ) for j in range(1, NZ)]
    for peer in peers:
        pl.semaphore_signal(barrier, inc=1, device_id=peer, device_id_type=MESH)

    loads = [
        pltpu.make_async_copy(src, dst, lsem.at[n])
        for n, (src, dst) in enumerate(
            (
                (rel_in, rel),
                (rid_in, rid),
                (x_in, x),
                (y_in, y),
                (yst_in, yst),
                (pos_in, pos),
                (xst_in, xst),
            )
        )
    ]
    for copy in loads:
        copy.start()
    gh[W:] = jnp.zeros((D - W, S), bf16)
    gl[W:] = jnp.zeros((D - W, S), bf16)
    for r in range(2):
        pad = r * HALF + MAIN
        acc[pad : pad + 10] = jnp.zeros((10, 8, 128), f32)
    b2[P2:] = jnp.zeros((P3 * NZ - P2, 8, 128), f32)
    loads[0].wait()
    rh[...], rl[...] = split(rel[...])
    loads[1].wait()
    loads[2].wait()
    xh[...], xl[...] = split(x[...])
    for copy in loads[3:]:
        copy.wait()
    for c in range(2):
        yin[0, c, :W] = y[:, c * C : (c + 1) * C]
        yin[0, c, W:] = jnp.broadcast_to(yst[:, c * C : (c + 1) * C], (8, C))

    def queries(k):
        r = rid[k]
        qh[...], ql[...] = split(dot3_rows(rh[r], rl[r], xh[...], xl[...]))

    def scores(k, arrived):
        for c in range(2):
            if arrived is not None:
                arrived[c].wait_recv()
            high, low = split(yin[k, c, :W])
            yh[:, c * C : (c + 1) * C] = high
            yl[:, c * C : (c + 1) * C] = low
            sc[c * C : (c + 1) * C] = dot3_rows(high, low, qh[...], ql[...])
        for n in range(3):
            part = slice(n * 256, (n + 1) * 256)
            s = sc[:, part]
            e = jnp.exp(s - jnp.max(s, axis=0, keepdims=True))
            chance = e * (1.0 / jnp.sum(e, axis=0, keepdims=True))
            rows = lax.broadcasted_iota(jnp.int32, (D, 256), 0)
            onehot = (rows == pos[k, :, part]).astype(f32)
            sh[:, part], sl[:, part] = split(chance - onehot)

    def new_targets(k, c):
        part = slice(c * C, (c + 1) * C)
        grad = dot3(qh[...], ql[...], sh[part], sl[part], 1, 1)
        rows, state = adagrad(yin[k, c, :W], yin[k, c, W : W + 1], grad)
        ysend[k, c, :W] = rows
        ysend[k, c, W:] = jnp.broadcast_to(state, (8, C))

    def target_copy(k, c):
        return pltpu.make_async_remote_copy(
            src_ref=ysend.at[k, c],
            dst_ref=yin.at[k + 1, c],
            send_sem=y_ssem.at[k, c],
            recv_sem=y_rsem.at[k, c],
            device_id=behind,
            device_id_type=MESH,
        )

    def send_targets(k, c):
        copy = target_copy(k, c)
        copy.start()
        return copy

    def query_grad():
        gh[:W], gl[:W] = split(dot3(yh[...], yl[...], sh[...], sl[...], 1, 0))

    def operator_grad(k, h, add):
        part = slice(h * 256, (h + 1) * 256)
        og = dot3(xh[...], xl[...], gh[part], gl[part], 1, 1)
        for r in range(2):
            mine = rid[k] == r
            for c in range(2 - h):
                to = pl.ds(r * HALF + (2 * h + c) * 50, 50)
                new = jnp.where(mine, og[:, c * 128 : (c + 1) * 128].reshape(50, 8, 128), 0.0)
                acc[to] = acc[to] + new if add else new
        if h == 0:
            return
        tail = og[:, 128:].T[:16]
        for r in range(2):
            mine = rid[k] == r
            for i in range(2):
                for c in range(4):
                    n = 128 if c < 3 else 16
                    t = r * HALF + MAIN + i * 4 + c
                    new = jnp.where(mine, tail[i * 8 : (i + 1) * 8, c * 128 : c * 128 + n], 0.0)
                    acc[t, :, :n] = acc[t, :, :n] + new if add else new

    def new_sources(k):
        r = rid[k]
        grad = dot3(rh[r], rl[r], gh[:W], gl[:W], 1, 0)
        rows, state = adagrad(x[...], xst[...], grad)
        x[...] = rows
        xst[...] = state
        xh[...], xl[...] = split(rows)

    def update(u, _):
        def send(number, src, dst, peer):
            copy = pltpu.make_async_remote_copy(
                src_ref=src,
                dst_ref=dst,
                send_sem=ssem.at[u, number],
                recv_sem=rsem.at[u, number],
                device_id=peer,
                device_id_type=MESH,
            )
            copy.start()
            return copy

        k = 2 * u
        queries(k)
        scores(k, None)
        new_targets(k, 0)

        @pl.when(u == 0)
        def _():
            pl.semaphore_wait(barrier, len(peers))

        moved = [send_targets(k, 0)]
        new_targets(k, 1)
        moved.append(send_targets(k, 1))
        query_grad()
        for h in range(2):
            operator_grad(k, h, False)
        new_sources(k)
        queries(k + 1)
        scores(k + 1, moved)

        def targets_of(which):
            @pl.when(core == which)
            def _():
                for c in range(2):
                    new_targets(k + 1, c)
                    send_targets(k + 1, c)

        targets_of(1)
        moved2 = [target_copy(k + 1, c) for c in range(2)]
        query_grad()

        sent = []
        for h in range(2):
            operator_grad(k + 1, h, True)
            start, size = (0, PART) if h == 0 else (PART, HALF - PART)
            theirs = pl.ds((1 - core) * HALF + start, size)
            sent.append(send(N_EX + h, acc.at[theirs], rx.at[u, pl.ds(start, size)], other))

        def chip_sum(p):
            r1[pl.ds(p * P1, P1)] = acc[pl.ds(core * HALF + p * P1, P1)] + rx[u, pl.ds(p * P1, P1)]

        for p in range(4):
            if p % 2 == 0:
                sent[p // 2].wait_recv()
            chip_sum(p)
        got = {}
        for t in (*RING_ORDER, 0):
            q = (second + t) % 4
            for j in RING_ORDER:
                p = (first + j) % 4
                src = r1.at[pl.ds(p * P1 + q * P2, P2)]
                n = 4 * (j - 1) + t
                got[j, t] = send(N_1 + n, src, b1.at[u, n], first_peer(p))
        sent += got.values()
        targets_of(0)
        new_sources(k + 1)

        def ring_sum(t):
            for j in ARRIVAL:
                got[j, t].wait_recv()
            own = r1[pl.ds(first * P1 + (second + t) % 4 * P2, P2)]
            return own + b1[u, t] + b1[u, 4 + t] + b1[u, 8 + t]

        got2 = []
        for t in RING_ORDER:
            r2[t] = ring_sum(t)
            got2.append(send(N_2 + t - 1, r2.at[t], r3.at[u, t - 1], second_peer((second + t) % 4)))
        sent += got2
        total = ring_sum(0)
        for copy in got2:
            copy.wait_recv()
        b2[:P2] = total + r3[u, 0] + r3[u, 1] + r3[u, 2]
        got = []
        for j in Z_ORDER:
            p = (my_z + j) % NZ
            got.append(send(N_3 + j - 1, b2.at[pl.ds(p * P3, P3)], g3.at[u, j], z_peer(p)))
        sent += got
        for copy in got:
            copy.wait_recv()
        total = b2[pl.ds(my_z * P3, P3)]
        for j in range(1, NZ):
            total = total + g3[u, j]
        g3[u, 0] = gradient_scale * total
        mine = pl.ds(my_z * P3, P3)
        g2[u, mine] = g3[u, 0]
        got = []
        for j in Z_ORDER:
            p = (my_z + j) % NZ
            got.append(send(N_4 + j - 1, g3.at[u, 0], g2.at[u, mine], z_peer(p)))
        sent += got
        for copy in got:
            copy.wait_recv()
        def place(f, s_):
            return pl.ds((core * 4 + f) * P1 + s_ * P2, P2)

        across, around = [], {}

        def cross(n, where):
            across.append(send(N_7 + n, gall.at[u, where], gall.at[u, where], other))

        def spread(t, where):
            for j in RING_ORDER:
                n = 4 * (j - 1) + t
                peer = first_peer((first + j) % 4)
                around[j, t] = send(N_6 + n, gall.at[u, where], gall.at[u, where], peer)

        mine = place(first, second)
        gall[u, mine] = g2[u, pl.ds(0, P2)]
        got2 = {}
        for j in RING_ORDER:
            peer = second_peer((second + j) % 4)
            got2[j] = send(N_5 + j - 1, gall.at[u, mine], gall.at[u, mine], peer)
        spread(0, mine)
        cross(0, mine)
        for t in ARRIVAL:
            got2[t].wait_recv()
            theirs = place(first, (second + 4 - t) % 4)
            spread(t, theirs)
            cross(t, theirs)
        for t in (0, *ARRIVAL):
            for j in ARRIVAL:
                around[j, t].wait_recv()
                cross(4 * j + t, place((first + 4 - j) % 4, (second + 4 - t) % 4))
        sent += [*got2.values(), *around.values(), *across]

        def apply(r):
            def store(start, end, values):
                rel[r, :, start:end] = rel[r, :, start:end] - operator_rate * values

            @pl.when(u == 0)
            def _():
                unpack(gall, u, r, store)
                rh[r], rl[r] = split(rel[r])

        apply(core)
        for copy in across:
            copy.wait_recv()
        apply(1 - core)
        for copy in moved + moved2 + sent:
            copy.wait_send()
        for copy in moved2:
            copy.wait_recv()
        return 0

    lax.fori_loop(0, STEPS // 2, update, 0)


def finish(x, xst, yin, gall, rel, x_out, xst_out, y_out, yst_out, rel_out, og_out, og, rel_new, sem):
    copies = [pltpu.make_async_copy(x, x_out, sem.at[0])]
    for c in range(2):
        part = pl.ds(c * C, C)
        rows = yin.at[STEPS, c, pl.ds(0, W)]
        copies.append(pltpu.make_async_copy(rows, y_out.at[:, part], sem.at[1 + c]))
    for copy in copies:
        copy.start()
    xst_out[...] = xst[...]
    for c in range(2):
        yst_out[:, c * C : (c + 1) * C] = yin[STEPS, c, W : W + 1]
    for r in range(2):
        for u in range(2):

            def store(start, end, values):
                og[u, r, :, start:end] = values
                before = rel[r, :, start:end] if u == 0 else rel_new[r, :, start:end]
                rel_new[r, :, start:end] = before - operator_rate * values

            unpack(gall, u, r, store)
            copies.append(pltpu.make_async_copy(og.at[u, r], og_out.at[u, r], sem.at[3 + 2 * u + r]))
            copies[-1].start()
        copies.append(pltpu.make_async_copy(rel_new.at[r], rel_out.at[r], sem.at[7 + r]))
        copies[-1].start()
    for copy in copies:
        copy.wait()


def shards(
    source_rows, source_state, target_rows, destination_state, positives, relation_ids, relations
):
    everyone = S * lax.axis_size("blk") * lax.axis_size("grp")
    gradient_scale = grad_gain / math.sqrt(everyone)
    vmem = pl.BlockSpec(memory_space=pltpu.VMEM)
    hbm = pl.BlockSpec(memory_space=pltpu.HBM)
    tiles = (8, 128)
    operands = (
        source_rows[0, 0],
        source_state[0],
        target_rows[0, 0],
        destination_state[0],
        positives[:, 0],
        relation_ids[:, 0, 0],
        relations,
    )
    source, source_state, target, grads = pl.pallas_call(
        functools.partial(kernel, gradient_scale),
        out_shape=(
            jax.ShapeDtypeStruct((W, S), f32),
            jax.ShapeDtypeStruct((1, S), f32),
            jax.ShapeDtypeStruct((STEPS + 1, 2, W + 8, C), f32),
            jax.ShapeDtypeStruct((2, TILES, *tiles), f32),
        ),
        in_specs=[hbm] * 7,
        out_specs=(vmem,) * 4,
        scratch_shapes=[
            pltpu.VMEM((W, D), f32),
            pltpu.VMEM((1, D), f32),
            pltpu.VMEM((STEPS, 1, S), jnp.int32),
            pltpu.SMEM((STEPS,), jnp.int32),
            pltpu.VMEM((2, W, W), f32),
            pltpu.VMEM((STEPS, 2, W + 8, C), f32),
            pltpu.VMEM((W, S), bf16),
            pltpu.VMEM((W, S), bf16),
            pltpu.VMEM((W, D), bf16),
            pltpu.VMEM((W, D), bf16),
            pltpu.VMEM((W, S), bf16),
            pltpu.VMEM((W, S), bf16),
            pltpu.VMEM((D, S), f32),
            pltpu.VMEM((D, S), bf16),
            pltpu.VMEM((D, S), bf16),
            pltpu.VMEM((D, S), bf16),
            pltpu.VMEM((D, S), bf16),
            pltpu.VMEM((2, W, W), bf16),
            pltpu.VMEM((2, W, W), bf16),
            pltpu.VMEM((TILES, *tiles), f32),
            pltpu.VMEM((2, HALF, *tiles), f32),
            pltpu.VMEM((HALF, *tiles), f32),
            pltpu.VMEM((2, 12, P2, *tiles), f32),
            pltpu.VMEM((4, P2, *tiles), f32),
            pltpu.VMEM((P3 * NZ, *tiles), f32),
            pltpu.VMEM((2, 3, P2, *tiles), f32),
            pltpu.VMEM((2, NZ, P3, *tiles), f32),
            pltpu.VMEM((2, P3 * NZ, *tiles), f32),
            pltpu.SemaphoreType.DMA((STEPS, 2)),
            pltpu.SemaphoreType.DMA((STEPS, 2)),
            pltpu.SemaphoreType.DMA((2, N_ALL)),
            pltpu.SemaphoreType.DMA((2, N_ALL)),
            pltpu.SemaphoreType.DMA((7,)),
        ],
        compiler_params=pltpu.CompilerParams(
            collective_id=0, has_side_effects=True, vmem_limit_bytes=36 << 20
        ),
        name="train",
    )(*(pltpu.with_memory_space_constraint(operand, pltpu.HBM) for operand in operands))
    out = pl.pallas_call(
        finish,
        out_shape=(
            jax.ShapeDtypeStruct((W, S), f32),
            jax.ShapeDtypeStruct((1, S), f32),
            jax.ShapeDtypeStruct((W, D), f32),
            jax.ShapeDtypeStruct((1, D), f32),
            jax.ShapeDtypeStruct((2, W, W), f32),
            jax.ShapeDtypeStruct((2, 2, W, W), f32),
        ),
        in_specs=[vmem] * 5,
        out_specs=(hbm, vmem, hbm, vmem, hbm, hbm),
        scratch_shapes=[
            pltpu.VMEM((2, 2, W, W), f32),
            pltpu.VMEM((2, W, W), f32),
            pltpu.SemaphoreType.DMA((9,)),
        ],
        compiler_params=pltpu.CompilerParams(vmem_limit_bytes=24 << 20),
        name="finish",
    )(source, source_state, target, grads, relations)
    source, source_state, target, target_state, relations, grads = out
    return (
        source[None, None],
        source_state[None],
        target[None, None],
        target_state[None],
        relations,
        grads,
    )


def solution(mesh):
    in_specs = (
        P("blk", "grp", None, None),
        P("blk", "grp", None),
        P("blk", "grp", None, None),
        P("blk", "grp", None),
        P(None, "blk", "grp", None),
        P(None, "blk", "grp"),
        P(),
    )
    out_specs = (
        P("blk", "grp", None, None),
        P("blk", "grp", None),
        P("blk", "grp", None, None),
        P("blk", "grp", None),
        P(),
        P(),
    )
    return jax.shard_map(shards, mesh=mesh, in_specs=in_specs, out_specs=out_specs, check_vma=False)
```
